512 devices in a mesh: gx: 32 (over x_lo, z, core), gy: 16 (over y, x_hi).
Axes of the slice: x: 4 (x_hi: 2, x_lo: 2; x = x_hi * 2 + x_lo), y: 8, z: 8, core: 2. Of those that a mesh axis runs over, the one named last changes fastest.
Arguments:
- u_field: float32 [1024, 4096], P('gx', 'gy'), may hold values from -6 to 6
- v_field: float32 [1024, 4096], P('gx', 'gy'), may hold values from -6 to 6
- w_first: bfloat16 [9, 64, 2], replicated, may hold values from -1.5 to 1.5
- b_first: float32 [64], replicated, may hold values from -3 to 3
- w_second: bfloat16 [9, 64, 64], replicated, may hold values from -0.25 to 0.25
- b_second: float32 [64], replicated, may hold values from -3 to 3
- w_third: bfloat16 [9, 16, 64], replicated, may hold values from -0.25 to 0.25
- b_third: float32 [16], replicated, may hold values from -3 to 3
Outputs:
- u_next: float32 [1024, 4096], P('gx', 'gy')
- v_next: float32 [1024, 4096], P('gx', 'gy')
The draws below stay inside these ranges and needn't reach their ends.
All inputs are finite; a program needn't handle non-finite values.
Results may differ from the reference program's by a relative error of at most 0.0023.
Values sent between devices are 32-bit elements; how exact they have to be, the bound alone decides.
A program may use at most 64 MiB of HBM per device.

```python
import math
import jax
import jax.numpy as jnp
from jax import lax

CX = 32
CH = 64
NOUT = 16
NX = 1024
NY = 4096
N_GX = 32


def levels(key, dims, pieces, least, top_value):
    loudness, own = 1.0, jax.random.fold_in(key, 6)
    for dim, blocks in pieces:
        draws = jnp.exp(jax.random.uniform(jax.random.fold_in(own, dim), (blocks,), jnp.float32, least / len(pieces), top_value / len(pieces)))
        loudness = loudness * jnp.repeat(draws, dims[dim] // blocks).reshape([-1 if axis == dim else 1 for axis in range(len(dims))])
    return loudness


def gaussian(stream_key, extent, width, reach, cuts=(), held_as=jnp.bfloat16):
    drawn = width * jax.random.normal(stream_key, extent, jnp.float32)
    if cuts:
        drawn = drawn * levels(stream_key, extent, cuts, -0.22, 0.18)
    return jnp.clip(drawn, -reach, reach).astype(held_as)


def setup_inputs(seed: int = 0) -> dict:
    key_of = jax.random.split(jax.random.key(seed), 9)
    return {
        "u_field": gaussian(key_of[0], (NX, NY), 1.0, 6.0, ((0, 32), (1, 16)), jnp.float32),
        "v_field": gaussian(key_of[1], (NX, NY), 1.0, 6.0, ((0, 32), (1, 16)), jnp.float32),
        "w_first": gaussian(key_of[2], (9, CH, 2), 18 ** -0.5, 1.5),
        "b_first": gaussian(key_of[3], (CH,), 0.5, 3.0, (), jnp.float32),
        "w_second": gaussian(key_of[4], (9, CH, CH), (9 * CH) ** -0.5, 0.25),
        "b_second": gaussian(key_of[5], (CH,), 0.5, 3.0, (), jnp.float32),
        "w_third": gaussian(key_of[6], (9, NOUT, CH), (9 * CH) ** -0.5, 0.25),
        "b_third": gaussian(key_of[7], (NOUT,), 0.5, 3.0, (), jnp.float32),
    }


step_ratio = 0.4
stencil_base = (-0.0625, 0.5625, 0.5625, -0.0625)


def conv_layer(inputs, kernel, offsets):
    weights = kernel.astype(jnp.float32).reshape(3, 3, kernel.shape[1], kernel.shape[2]).transpose(2, 3, 0, 1)
    output = lax.conv_general_dilated(inputs.astype(jnp.float32)[None], weights, (1, 1), "VALID", dimension_numbers=("NCHW", "OIHW", "NCHW"), precision=lax.Precision.HIGHEST)[0]
    return output + offsets[:, None, None]


def shifted(values, shift_down, shift_right):
    return jnp.roll(values, (-shift_down, -shift_right), axis=(1, 2))


def wavenumber(counter, whole):
    signed = jnp.where(counter >= whole // 2, counter - whole, counter)
    return signed.astype(jnp.float32) * (2.0 * math.pi / whole)


def reference(u_field, v_field, w_first, b_first, w_second, b_second, w_third, b_third):
    field = jnp.stack([u_field, v_field])
    features = jnp.pad(field.astype(jnp.bfloat16), ((0, 0), (3, 3), (3, 3)), mode="wrap")

    def band(position):
        inputs = lax.dynamic_slice_in_dim(features, position * CX, CX + 6, axis=1)
        first = jax.nn.relu(conv_layer(inputs, w_first, b_first)).astype(jnp.bfloat16)
        second = jax.nn.relu(conv_layer(first, w_second, b_second)).astype(jnp.bfloat16)
        return conv_layer(second, w_third, b_third)

    coeff = lax.map(band, jnp.arange(N_GX, dtype=jnp.int32))
    coeff = jnp.transpose(coeff, (1, 0, 2, 3)).reshape(NOUT, NX, NY)
    weights = coeff.reshape(2, 2, 4, NX, NY)
    weights = jnp.asarray(stencil_base, jnp.float32)[:, None, None] + weights - jnp.mean(weights, axis=2, keepdims=True)
    east = weights[0, :, 0] * shifted(field, -1, 0) + weights[0, :, 1] * field + weights[0, :, 2] * shifted(field, 1, 0) + weights[0, :, 3] * shifted(field, 2, 0)
    north = weights[1, :, 0] * shifted(field, 0, -1) + weights[1, :, 1] * field + weights[1, :, 2] * shifted(field, 0, 1) + weights[1, :, 3] * shifted(field, 0, 2)
    carry_x = 0.5 * (field[0] + shifted(field, 1, 0)[0])
    carry_y = 0.5 * (field[1] + shifted(field, 0, 1)[1])
    flow_x = carry_x * east
    flow_y = carry_y * north
    star = field - step_ratio * (flow_x - shifted(flow_x, -1, 0) + flow_y - shifted(flow_y, 0, -1))
    spectra = jnp.fft.fft2(star, axes=(1, 2))
    wave_x = wavenumber(jnp.arange(NX, dtype=jnp.int32), NX)[:, None]
    wave_y = wavenumber(jnp.arange(NY, dtype=jnp.int32), NY)[None, :]
    denominator = wave_x * wave_x + wave_y * wave_y
    denominator = jnp.where(denominator == 0, 1.0, denominator)
    share = (wave_x * spectra[0] + wave_y * spectra[1]) / denominator
    projected = jnp.stack([spectra[0] - wave_x * share, spectra[1] - wave_y * share])
    result = jnp.fft.ifft2(projected, axes=(1, 2)).real
    return result[0].astype(jnp.float32), result[1].astype(jnp.float32)
```

```python
import functools
import math

import jax
import jax.numpy as jnp
import ml_dtypes
import numpy as np
from jax import lax
from jax.experimental import pallas as pl
from jax.experimental.pallas import tpu as pltpu
from jax.sharding import PartitionSpec as P

step_ratio = 0.4
stencil_base = (-0.0625, 0.5625, 0.5625, -0.0625)
block_height = 8
GX = 32
GY = 16
NX = 1024
NY = 4096
f32 = jnp.float32
bf16 = jnp.bfloat16


def padded_2(value, sides, width):
    for axis, dim in sides:
        peers, length = (lax.axis_size(axis), value.shape[dim])
        up = [(i, (i + 1) % peers) for i in range(peers)]
        down = [(j, i) for i, j in up]
        last = lax.slice_in_dim(value, length - width, length, axis=dim)
        first = lax.slice_in_dim(value, 0, width, axis=dim)
        before = lax.ppermute(last, axis, up)
        after = lax.ppermute(first, axis, down)
        value = jnp.concatenate([before, value, after], axis=dim)
    return value


def from_behind(block, axis, distance):
    devices = range(lax.axis_size(axis))
    route = [((i - distance) % len(devices), i) for i in devices]
    return lax.ppermute(block, axis, route)


def convolve(inputs, kernel, offsets, height, breadth):
    summed = None
    for tap_index in range(9):
        shift_down = tap_index // 3
        shift_right = tap_index % 3
        window = inputs[:, shift_down : shift_down + height, shift_right : shift_right + breadth]
        term = jnp.einsum(
            "oc,chw->ohw", kernel[tap_index], window, preferred_element_type=jnp.float32
        )
        summed = term if summed is None else summed + term
    return summed + offsets[:, None, None]


def predict(features, layers, top_row, left_col, height, breadth):
    w_first, b_first, w_second, b_second, w_third, b_third = layers
    inputs = lax.dynamic_slice(
        features, (0, top_row, left_col), (features.shape[0], height + 6, breadth + 6)
    )
    first = jax.nn.relu(convolve(inputs, w_first, b_first, height + 4, breadth + 4)).astype(
        jnp.bfloat16
    )
    second = jax.nn.relu(convolve(first, w_second, b_second, height + 2, breadth + 2)).astype(
        jnp.bfloat16
    )
    return convolve(second, w_third, b_third, height, breadth)


def coefficients(features, layers, margin, first_col, breadth):
    height = features.shape[1] - 2 * margin
    initial = jnp.zeros((layers[4].shape[1], height, breadth), jnp.float32)

    def advance(position, outputs):
        start_row = position * block_height
        piece = predict(
            features, layers, start_row + margin - 3, margin - 3 + first_col, block_height, breadth
        )
        return lax.dynamic_update_slice(outputs, piece, (0, start_row, 0))

    return lax.fori_loop(0, height // block_height, advance, initial)


def fluxes(padded, coeff, margin, anchor, height, breadth):

    def sample(shift_down, shift_right):
        top_row = margin + anchor + shift_down
        left_col = margin + anchor + shift_right
        return padded[:, top_row : top_row + height, left_col : left_col + breadth]

    weights = coeff.reshape(2, 2, 4, height, breadth)
    weights = (
        jnp.asarray(stencil_base, jnp.float32)[:, None, None]
        + weights
        - jnp.mean(weights, axis=2, keepdims=True)
    )
    centre = sample(0, 0)
    east = (
        weights[0, :, 0] * sample(-1, 0)
        + weights[0, :, 1] * centre
        + weights[0, :, 2] * sample(1, 0)
        + weights[0, :, 3] * sample(2, 0)
    )
    north = (
        weights[1, :, 0] * sample(0, -1)
        + weights[1, :, 1] * centre
        + weights[1, :, 2] * sample(0, 1)
        + weights[1, :, 3] * sample(0, 2)
    )
    carry_x = 0.5 * (centre[0] + sample(1, 0)[0])
    carry_y = 0.5 * (centre[1] + sample(0, 1)[1])
    return (carry_x * east, carry_y * north)


def star_fields(u_field, v_field, layers):
    field = jnp.stack([u_field, v_field])
    height, breadth = u_field.shape
    padded = padded_2(field, (("gx", 1), ("gy", 2)), 3)
    features = padded.astype(jnp.bfloat16)
    coeff = coefficients(features, layers, 3, 0, breadth)
    east_now, north_now = fluxes(padded, coeff, 3, 0, height, breadth)
    below = from_behind(east_now[:, -1:, :], "gx", 1)
    beside = from_behind(north_now[:, :, -1:], "gy", 1)
    east_before = jnp.concatenate([below, east_now[:, :-1]], axis=1)
    north_before = jnp.concatenate([beside, north_now[:, :, :-1]], axis=2)
    return field - step_ratio * (east_now - east_before + north_now - north_before)


def split_bf16(table):
    hi = table.astype(np.float32).astype(ml_dtypes.bfloat16)
    lo = (table - hi.astype(np.float64)).astype(np.float32).astype(ml_dtypes.bfloat16)
    return hi, lo


def real_left(matrix):
    return np.block([[matrix.real, -matrix.imag], [matrix.imag, matrix.real]])


def triple_left(table):
    hi, lo = split_bf16(table)
    return np.concatenate([hi, hi, lo], axis=1)


def root(product, whole):
    return np.exp(-2j * np.pi * (product % whole) / whole)


@functools.cache
def tables():
    n16, n32, n256 = np.arange(16), np.arange(32), np.arange(256)
    paired = np.concatenate([2 * n16, 2 * n16 + 1])
    dft16 = real_left(root(np.outer(n16, n16), 16))
    conj_in = np.concatenate([np.ones(16), -np.ones(16)])
    t_a = triple_left(dft16 * conj_in[None, :])
    t_a2 = triple_left(dft16 * conj_in[:, None])
    mid = root(np.outer(n256, n256), 256)
    t_b = np.stack(split_bf16(np.block([[mid.real, mid.imag], [-mid.imag, mid.real]])))
    tw = root(np.outer(n16, n256), 4096)
    tw = np.stack([tw.real, tw.imag]).astype(np.float32)
    t_r = triple_left(real_left(root(np.outer(paired, n32), 32)))
    t_r2 = triple_left(real_left(root(np.outer(n32, paired), 32)))
    t_p = triple_left(real_left(root(np.outer(n32, paired), 32)))
    t_p2 = triple_left(real_left(root(np.outer(paired, n32), 32)))
    t_s = np.stack([t_r, t_r2, t_p, t_p2])
    twr = np.zeros((16, 32, 4), np.float32)
    for r in range(2):
        row = root(np.outer(2 * n16 + r, paired), 1024)
        twr[:, :, 2 * r] = row.real
        twr[:, :, 2 * r + 1] = row.imag
    return np.stack([t_a, t_a2]), t_b, tw, t_s, twr


def triple(value):
    hi = value.astype(bf16)
    lo = (value - hi.astype(f32)).astype(bf16)
    return jnp.concatenate([hi, lo, hi], axis=0)


def left_product(table, value):
    return jnp.dot(table, triple(value), preferred_element_type=f32)


def right_product(value, t_b):
    rows = value.shape[0]
    hi = value.astype(bf16)
    lo = (value - hi.astype(f32)).astype(bf16)
    both = jnp.dot(jnp.concatenate([hi, lo], axis=0), t_b[0], preferred_element_type=f32)
    return both[:rows] + both[rows:] + jnp.dot(hi, t_b[1], preferred_element_type=f32)


def spectral_kernel(star, t_a, t_b, tw, t_s, twr, out, st, s1, r1, s2, r2, s3, r3, s4, r4, s5, r5, s6, r6, ssem, rsem):
    a = lax.axis_index("gx")
    b = lax.axis_index("gy")
    MESH = pl.DeviceIdType.MESH

    barrier = pltpu.get_barrier_semaphore()

    def greet_x(d, _):
        pl.semaphore_signal(barrier, inc=1, device_id={"gx": (a + d) % GX}, device_id_type=MESH)
        return 0

    def greet_y(d, _):
        pl.semaphore_signal(barrier, inc=1, device_id={"gy": (b + d) % GY}, device_id_type=MESH)
        return 0

    lax.fori_loop(1, GX, greet_x, 0)
    lax.fori_loop(1, GY, greet_y, 0)
    pl.semaphore_wait(barrier, GX + GY - 2)

    def far_first(step, size):
        half = (step + 1) // 2
        return size // 2 + half - 2 * half * (step % 2)

    def send_y(stage, src, dst):
        def go(step, _):
            peer = (b + far_first(step, GY)) % GY
            pltpu.make_async_remote_copy(
                src.at[peer], dst.at[b], ssem.at[stage], rsem.at[stage],
                device_id={"gy": peer}, device_id_type=MESH,
            ).start()
            return 0

        lax.fori_loop(0, GY - 1, go, 0)
        dst[b] = src[b]

    def send_x(stage, src_of, dst_of):
        def go(step, _):
            peer = (a + far_first(step, GX)) % GX
            pltpu.make_async_remote_copy(
                src_of(peer), dst_of(a), ssem.at[stage], rsem.at[stage],
                device_id={"gx": peer}, device_id_type=MESH,
            ).start()
            return 0

        lax.fori_loop(0, GX - 1, go, 0)

    def wait_for(sem, like):
        pltpu.make_async_copy(like, like, sem).wait()

    for c in range(2):
        for h in range(2):
            st[c * 2 + h] = star[c, :, h * 128 : h * 128 + 128]
    for c in range(2):
        for r in range(2):
            for h in range(2):
                s1[:, c * 4 + r * 2 + h, :] = st[c * 2 + h, pl.ds(r, 16, stride=2), :]
    send_y(0, s1, r1)

    shape = (32, 256)
    m2 = lax.broadcasted_iota(jnp.int32, shape, 0)
    lane = lax.broadcasted_iota(jnp.int32, shape, 1)
    kx = 2 * b + lane // 128 + 32 * m2
    ky = a // 2 + 16 * ((a % 2) * 128 + lane % 128)
    wx = jnp.where(kx >= NX // 2, kx - NX, kx).astype(f32) * (2.0 * math.pi / NX)
    wy = jnp.where(ky >= NY // 2, ky - NY, ky).astype(f32) * (2.0 * math.pi / NY)
    den = wx * wx + wy * wy
    origin = (kx == 0) & (ky == 0)
    den = jnp.where(origin, 1.0, den)
    scale = 1.0 / (NX * NY)
    share = scale / den
    g_re = 0.5 * (wy * wy - wx * wx) * share
    g_im = -(wx * wy) * share
    g_im = jnp.where((kx == NX // 2) != (ky == NY // 2), 0.0, g_im)
    g_one = jnp.where(origin, 0.5 * scale, g_re)
    g_two = jnp.where(origin, -0.5 * scale, g_re)

    wait_for(rsem.at[0], r1.at[pl.ds(0, GY - 1)])

    tr, ti = tw[0], tw[1]
    x = jnp.concatenate(
        [
            jnp.concatenate([r1[:, c * 4 + k, :] for k in range(4)], axis=1)
            for c in range(2)
        ],
        axis=0,
    )
    y = left_product(t_a[0], x)
    lines = []
    for r in range(2):
        yr, yi = y[:16, r * 256 : r * 256 + 256], y[16:, r * 256 : r * 256 + 256]
        lines.append(jnp.concatenate([yr * tr - yi * ti, yr * ti + yi * tr], axis=1))
    o = right_product(jnp.concatenate(lines, axis=0), t_b)
    for c in range(2):
        for r in range(2):
            for h in range(2):
                at = c * 256 + h * 128
                s2[:, h, c * 2 + r, :] = o[r * 16 : r * 16 + 16, at : at + 128]
    send_x(1, lambda peer: s2.at[peer // 2, peer % 2], lambda me: r2.at[me])
    r2[a] = s2[a // 2, a % 2]
    wait_for(rsem.at[1], r2.at[pl.ds(0, GX - 1)])

    x = jnp.concatenate(
        [jnp.concatenate([r2[:, c * 2 + r, :] for r in range(2)], axis=1) for c in range(2)], axis=0
    )
    y = left_product(t_s[0], x)
    column = twr[b]
    for r in range(2):
        cr, ci = column[:, 2 * r : 2 * r + 1], column[:, 2 * r + 1 : 2 * r + 2]
        yr, yi = y[:32, r * 128 : r * 128 + 128], y[32:, r * 128 : r * 128 + 128]
        for c, value in enumerate((yr * cr - yi * ci, yr * ci + yi * cr)):
            for t in range(2):
                s3[:, c * 4 + r * 2 + t, :] = value[t * 16 : t * 16 + 16]
    send_y(2, s3, r3)
    wait_for(rsem.at[2], r3.at[pl.ds(0, GY - 1)])
    x = jnp.concatenate(
        [
            jnp.concatenate([r3[:, c * 4 + r * 2 + t, :] for t in range(2)], axis=1)
            for c in range(2)
            for r in range(2)
        ],
        axis=0,
    )
    y = left_product(t_s[2], x)
    yr, yi = y[:32], y[32:]

    q = jnp.concatenate([g_one * yr - g_im * yi, -(g_two * yi + g_im * yr)], axis=0)

    y = left_product(t_s[3], q)
    for c in range(2):
        for r in range(2):
            for t in range(2):
                row = c * 32 + r * 16
                s4[:, c * 4 + r * 2 + t, :] = y[row : row + 16, t * 128 : t * 128 + 128]
    send_y(3, s4, r4)
    wait_for(rsem.at[3], r4.at[pl.ds(0, GY - 1)])
    halves = [[], []]
    for r in range(2):
        cr, ci = column[:, 2 * r : 2 * r + 1], column[:, 2 * r + 1 : 2 * r + 2]
        yr, yi = (
            jnp.concatenate([r4[:, c * 4 + r * 2 + t, :] for t in range(2)], axis=0) for c in range(2)
        )
        halves[0].append(yr * cr - yi * ci)
        halves[1].append(yr * ci + yi * cr)
    x = jnp.concatenate([jnp.concatenate(half, axis=1) for half in halves], axis=0)
    y = left_product(t_s[1], x)
    for c in range(2):
        for r in range(2):
            s5[:, c * 2 + r, :] = y[c * 32 : c * 32 + 32, r * 128 : r * 128 + 128]
    send_x(4, lambda peer: s5.at[peer], lambda me: r5.at[me // 2, me % 2])
    r5[a // 2, a % 2] = s5[a]
    wait_for(rsem.at[4], s5.at[pl.ds(0, GX - 1)])
    x = jnp.concatenate(
        [
            jnp.concatenate([r5[:, h, c * 2 + r, :] for c in range(2) for h in range(2)], axis=1)
            for r in range(2)
        ],
        axis=0,
    )
    o = right_product(x, t_b)
    lines = [[], []]
    for r in range(2):
        yr, yi = o[r * 16 : r * 16 + 16, :256], o[r * 16 : r * 16 + 16, 256:]
        lines[0].append(yr * tr - yi * ti)
        lines[1].append(yr * ti + yi * tr)
    x = jnp.concatenate([jnp.concatenate(line, axis=1) for line in lines], axis=0)
    y = left_product(t_a[1], x)
    for c in range(2):
        for k in range(4):
            s6[:, c * 4 + k, :] = y[c * 16 : c * 16 + 16, k * 128 : k * 128 + 128]
    send_y(5, s6, r6)
    wait_for(rsem.at[5], r6.at[pl.ds(0, GY - 1)])
    for c in range(2):
        for r in range(2):
            for h in range(2):
                st[c * 2 + h, pl.ds(r, 16, stride=2), :] = r6[:, c * 4 + r * 2 + h, :]
    for c in range(2):
        for h in range(2):
            lanes = slice(h * 128, h * 128 + 128)
            out[c, :, lanes] = 0.5 * star[c, :, lanes] + st[c * 2 + h]

    for stage, buffer in ((0, s1), (2, s3), (3, s4), (5, s6)):
        wait_for(ssem.at[stage], buffer.at[pl.ds(0, GY - 1)])
    wait_for(ssem.at[1], r2.at[pl.ds(0, GX - 1)])
    wait_for(ssem.at[4], s5.at[pl.ds(0, GX - 1)])


def project(star):
    whole = pl.BlockSpec(memory_space=pltpu.VMEM)
    y_buf = pltpu.VMEM((16, 8, 128), f32)
    x_buf = pltpu.VMEM((32, 4, 128), f32)
    pair_buf = pltpu.VMEM((16, 2, 4, 128), f32)
    t_a, t_b, tw, t_s, twr = (jnp.asarray(t) for t in tables())
    return pl.pallas_call(
        spectral_kernel,
        out_shape=jax.ShapeDtypeStruct((2, 32, 256), f32),
        in_specs=[whole] * 6,
        out_specs=whole,
        scratch_shapes=[
            pltpu.VMEM((4, 32, 128), f32),
            y_buf, y_buf, pair_buf, x_buf, y_buf, y_buf, y_buf, y_buf, x_buf, pair_buf, y_buf, y_buf,
            pltpu.SemaphoreType.DMA((6,)),
            pltpu.SemaphoreType.DMA((6,)),
        ],
        compiler_params=pltpu.CompilerParams(collective_id=0, has_side_effects=True),
        name="spectral",
    )(star, t_a, t_b, tw, t_s, twr)


def on_device(u_field, v_field, w_first, b_first, w_second, b_second, w_third, b_third):
    layers = (w_first, b_first, w_second, b_second, w_third, b_third)
    star = star_fields(u_field, v_field, layers)
    result = project(star)
    return result[0], result[1]


def solution(mesh):
    return jax.shard_map(
        on_device,
        mesh=mesh,
        in_specs=(P("gx", "gy"), P("gx", "gy"), P(), P(), P(), P(), P(), P()),
        out_specs=(P("gx", "gy"), P("gx", "gy")),
        check_vma=False,
    )
```

```python
import functools
import math

import jax
import jax.numpy as jnp
import ml_dtypes
import numpy as np
from jax import lax
from jax.experimental import pallas as pl
from jax.experimental.pallas import tpu as pltpu
from jax.sharding import PartitionSpec as P

step_ratio = 0.4
stencil_base = (-0.0625, 0.5625, 0.5625, -0.0625)
GX = 32
GY = 16
NX = 1024
NY = 4096
f32 = jnp.float32
bf16 = jnp.bfloat16


PITCH = 272
SHIFTS = (4, 3, 2, 1, 0, -1)


def nt(left, right):
    return lax.dot_general(left, right, (((1,), (1,)), ((), ())), preferred_element_type=f32)


def front_kernel(
    u, v, w1, b1, w2, b2, w3, b3, out,
    rows_in, cols_in, corner_in, fs, k1, k2, k3, x1, x2, cf, fx, ssem, rsem,
):
    a = lax.axis_index("gx")
    b = lax.axis_index("gy")
    MESH = pl.DeviceIdType.MESH
    moves = [(dx, dy) for dx in (-1, 0, 1) for dy in (-1, 0, 1) if (dx, dy) != (0, 0)]

    def at(dx, dy):
        return {"gx": (a + dx + GX) % GX, "gy": (b + dy + GY) % GY}

    barrier = pltpu.get_barrier_semaphore()
    for dx, dy in moves:
        pl.semaphore_signal(barrier, inc=1, device_id=at(dx, dy), device_id_type=MESH)
    pl.semaphore_wait(barrier, len(moves))

    copies = []
    for n, (dx, dy) in enumerate(moves):
        rows = {-1: slice(0, 8), 0: slice(0, 32), 1: slice(24, 32)}[dx]
        cols = {-1: slice(0, 128), 0: slice(0, 256), 1: slice(128, 256)}[dy]
        for c, field in enumerate((u, v)):
            if dx and dy:
                dst = corner_in.at[(dx + 1) // 2, (dy + 1) // 2, c]
            elif dx:
                dst = rows_in.at[(dx + 1) // 2, c]
            else:
                dst = cols_in.at[(dy + 1) // 2, c]
            copy = pltpu.make_async_remote_copy(
                field.at[rows, cols], dst, ssem.at[2 * n + c], rsem.at[2 * n + c],
                device_id=at(dx, dy), device_id_type=MESH,
            )
            copy.start()
            copies.append(copy)

    k1[...] = jnp.zeros_like(k1)
    k2[...] = jnp.zeros_like(k2)
    k3[...] = jnp.zeros_like(k3)
    for dj in range(3):
        for dr in range(3):
            tap = 3 * dr + dj
            for o in range(4):
                x = o + dr
                for c in range(2):
                    k1[(dj * 2 + c) * 8 + x : (dj * 2 + c) * 8 + x + 1, o * 64 : o * 64 + 64] = w1[
                        tap, c : c + 1, :
                    ].astype(f32)
                k2[dj, o * 64 : o * 64 + 64, x * 64 : x * 64 + 64] = w2[tap]
                k3[dj * 64 + o * 16 : dj * 64 + o * 16 + 16, x * 64 : x * 64 + 64] = w3[tap]
    bias1 = jnp.concatenate([b1[...]] * 4, axis=1)
    bias2 = jnp.concatenate([b2[...]] * 4, axis=1)
    x1[:, pl.ds(10 * PITCH, 16), :] = jnp.zeros((2, 16, 128), f32)
    x2[pl.ds(9 * PITCH, 384), :] = jnp.zeros((384, 256), bf16)

    for copy in copies:
        copy.wait()

    lane = lax.broadcasted_iota(jnp.int32, (8, 128), 1)
    for c, field in enumerate((u, v)):
        for g in range(6):
            if g in (0, 5):
                e = 1 if g == 0 else 0
                tiles = [
                    corner_in[e, 1, c], rows_in[e, c, :, 0:128], rows_in[e, c, :, 128:256], corner_in[e, 0, c],
                ]
            else:
                rows = slice(g * 8 - 8, g * 8)
                tiles = [
                    cols_in[1, c, rows, :], field[rows, 0:128], field[rows, 128:256], cols_in[0, c, rows, :],
                ]
            for n, s in enumerate(SHIFTS):
                if s == 0:
                    for k in range(3):
                        fs[n, c, k, g * 8 : g * 8 + 8, :] = tiles[k + 1]
                    continue
                turned = [pltpu.roll(tile, s % 128, 1) for tile in tiles]
                for k in range(3):
                    if s > 0:
                        value = jnp.where(lane < s, turned[k], turned[k + 1])
                    elif k < 2:
                        value = jnp.where(lane >= 128 + s, turned[k + 2], turned[k + 1])
                    else:
                        value = turned[k + 1]
                    fs[n, c, k, g * 8 : g * 8 + 8, :] = value

    def layer_1(i, _):
        patch = jnp.concatenate(
            [
                jnp.concatenate([fs[dj, c, k, pl.ds(4 * i + 4, 8), :] for k in range(3)], axis=1)
                for dj in range(3)
                for c in range(2)
            ],
            axis=0,
        ).astype(bf16)
        y = lax.dot_general(
            patch, k1[...].astype(bf16), (((0,), (0,)), ((), ())), preferred_element_type=f32
        )
        y = jnp.maximum(y[:PITCH] + bias1, 0.0)
        start = pl.multiple_of(i * PITCH, 8)
        x1[0, pl.ds(start, PITCH), :] = y[:, :128]
        x1[1, pl.ds(start, PITCH), :] = y[:, 128:]
        return 0

    lax.fori_loop(0, 10, layer_1, 0)

    CHUNK = 3 * PITCH

    def layer_2(i, _):
        start = i * CHUNK

        def piece(half, offset):
            return x1[half, pl.ds(start + offset, CHUNK), :].astype(bf16)

        y = None
        for dj in range(3):
            left = jnp.concatenate([piece(0, dj), piece(1, dj)], axis=1)
            term = nt(left, k2[dj, :, 0:256])
            y = term if y is None else y + term
        left = jnp.concatenate([piece(0, PITCH), piece(0, PITCH + 1)], axis=1)
        y = y + nt(left, jnp.concatenate([k2[0, :, 256:384], k2[1, :, 256:384]], axis=1))
        y = y + nt(piece(0, PITCH + 2), k2[2, :, 256:384])
        y = jnp.maximum(y + bias2, 0.0).astype(bf16)
        x2[pl.ds(pl.multiple_of(start, 16), CHUNK), :] = y
        return 0

    lax.fori_loop(0, 3, layer_2, 0)

    def layer_3(i, _):
        start = pl.multiple_of(i * PITCH, 16)
        after = pl.multiple_of((i + 1) * PITCH, 16)
        y = nt(k3[:, 0:256], x2[pl.ds(start, 384), :]) + nt(k3[:, 256:384], x2[pl.ds(after, 384), 0:128])
        y = y[0:64] + pltpu.roll(y[64:128], 383, 1) + pltpu.roll(y[128:192], 382, 1)
        for o in range(4):
            for k in range(3):
                cf[k, pl.ds(4 * i + o, 16, stride=40), :] = y[o * 16 : o * 16 + 16, k * 128 : k * 128 + 128]
        return 0

    lax.fori_loop(0, 9, layer_3, 0)

    def field_at(c, s, down, k, count=40):
        return fs[SHIFTS.index(s), c, k, pl.ds(7 + down, count), :]

    stepped = [[None] * 3 for _ in range(2)]
    for k in range(3):
        carry_x = 0.5 * (field_at(0, 1, 0, k) + field_at(0, 1, 1, k))
        carry_y = 0.5 * (field_at(1, 1, 0, k) + field_at(1, 0, 0, k))
        for q in range(2):
            flows = []
            for d in range(2):
                taps = (
                    [field_at(q, 1, down, k) for down in (-1, 0, 1, 2)]
                    if d == 0
                    else [field_at(q, s, 0, k) for s in (2, 1, 0, -1)]
                )
                weights = [
                    cf[k, (8 * d + 4 * q + s) * 40 : (8 * d + 4 * q + s) * 40 + 40, :] + b3[8 * d + 4 * q + s]
                    for s in range(4)
                ]
                mean = 0.25 * ((weights[0] + weights[1]) + (weights[2] + weights[3]))
                total = None
                for s in range(4):
                    term = (stencil_base[s] + weights[s] - mean) * taps[s]
                    total = term if total is None else total + term
                flows.append((carry_x if d == 0 else carry_y) * total)
            fx[0, q, k] = flows[0]
            fx[1, q, k] = flows[1]
    for q in range(2):
        along_y = jnp.concatenate([fx[1, q, k, pl.ds(1, 32), :] for k in range(3)], axis=1)
        along_x = jnp.concatenate(
            [fx[0, q, k, pl.ds(1, 32), :] - fx[0, q, k, pl.ds(0, 32), :] for k in range(3)], axis=1
        )
        here = jnp.concatenate([field_at(q, 1, 1, k, 32) for k in range(3)], axis=1)
        moved = here - step_ratio * (along_x + along_y - pltpu.roll(along_y, 1, 1))
        moved = pltpu.roll(moved, 383, 1)
        for h in range(2):
            out[q * 2 + h] = moved[:, h * 128 : h * 128 + 128]


def star_fields(u_field, v_field, layers):
    w_first, b_first, w_second, b_second, w_third, b_third = layers
    whole = pl.BlockSpec(memory_space=pltpu.VMEM)
    return pl.pallas_call(
        front_kernel,
        out_shape=jax.ShapeDtypeStruct((4, 32, 128), f32),
        in_specs=[whole] * 7 + [pl.BlockSpec(memory_space=pltpu.SMEM)],
        out_specs=whole,
        scratch_shapes=[
            pltpu.VMEM((2, 2, 8, 256), f32),
            pltpu.VMEM((2, 2, 32, 128), f32),
            pltpu.VMEM((2, 2, 2, 8, 128), f32),
            pltpu.VMEM((6, 2, 3, 56, 128), f32),
            pltpu.VMEM((48, 256), f32),
            pltpu.VMEM((3, 256, 384), bf16),
            pltpu.VMEM((192, 384), bf16),
            pltpu.VMEM((2, 10 * PITCH + 16, 128), f32),
            pltpu.VMEM((9 * PITCH + 384, 256), bf16),
            pltpu.VMEM((3, 640, 128), f32),
            pltpu.VMEM((2, 2, 3, 40, 128), f32),
            pltpu.SemaphoreType.DMA((16,)),
            pltpu.SemaphoreType.DMA((16,)),
        ],
        compiler_params=pltpu.CompilerParams(collective_id=1, has_side_effects=True),
        name="advect",
    )(
        u_field, v_field, jnp.transpose(w_first, (0, 2, 1)), b_first[None], w_second, b_second[None],
        w_third, b_third,
    )


def split_bf16(table):
    hi = table.astype(np.float32).astype(ml_dtypes.bfloat16)
    lo = (table - hi.astype(np.float64)).astype(np.float32).astype(ml_dtypes.bfloat16)
    return hi, lo


def real_left(matrix):
    return np.block([[matrix.real, -matrix.imag], [matrix.imag, matrix.real]])


def triple_left(table):
    hi, lo = split_bf16(table)
    return np.concatenate([hi, hi, lo], axis=1)


def root(product, whole):
    return np.exp(-2j * np.pi * (product % whole) / whole)


@functools.cache
def tables():
    n16, n32, n256 = np.arange(16), np.arange(32), np.arange(256)
    paired = np.concatenate([2 * n16, 2 * n16 + 1])
    dft16 = real_left(root(np.outer(n16, n16), 16))
    conj_in = np.concatenate([np.ones(16), -np.ones(16)])
    t_a = triple_left(dft16 * conj_in[None, :])
    t_a2 = triple_left(dft16 * conj_in[:, None])
    mid = root(np.outer(n256, n256), 256)
    t_b = np.stack(split_bf16(np.block([[mid.real, mid.imag], [-mid.imag, mid.real]])))
    tw = root(np.outer(n16, n256), 4096)
    tw = np.stack([tw.real, tw.imag]).astype(np.float32)
    t_r = triple_left(real_left(root(np.outer(paired, n32), 32)))
    t_r2 = triple_left(real_left(root(np.outer(n32, paired), 32)))
    t_p = triple_left(real_left(root(np.outer(n32, paired), 32)))
    t_p2 = triple_left(real_left(root(np.outer(paired, n32), 32)))
    t_s = np.stack([t_r, t_r2, t_p, t_p2])
    twr = np.zeros((16, 32, 4), np.float32)
    for r in range(2):
        row = root(np.outer(2 * n16 + r, paired), 1024)
        twr[:, :, 2 * r] = row.real
        twr[:, :, 2 * r + 1] = row.imag
    return np.stack([t_a, t_a2]), t_b, tw, t_s, twr


def triple(value):
    hi = value.astype(bf16)
    lo = (value - hi.astype(f32)).astype(bf16)
    return jnp.concatenate([hi, lo, hi], axis=0)


def left_product(table, value):
    return jnp.dot(table, triple(value), preferred_element_type=f32)


def right_product(value, t_b):
    rows = value.shape[0]
    hi = value.astype(bf16)
    lo = (value - hi.astype(f32)).astype(bf16)
    both = jnp.dot(jnp.concatenate([hi, lo], axis=0), t_b[0], preferred_element_type=f32)
    return both[:rows] + both[rows:] + jnp.dot(hi, t_b[1], preferred_element_type=f32)


def spectral_kernel(star, t_a, t_b, tw, t_s, twr, out, st, s1, r1, s2, r2, s3, r3, s4, r4, s5, r5, s6, r6, ssem, rsem):
    a = lax.axis_index("gx")
    b = lax.axis_index("gy")
    MESH = pl.DeviceIdType.MESH

    barrier = pltpu.get_barrier_semaphore()

    def greet_x(d, _):
        pl.semaphore_signal(barrier, inc=1, device_id={"gx": (a + d) % GX}, device_id_type=MESH)
        return 0

    def greet_y(d, _):
        pl.semaphore_signal(barrier, inc=1, device_id={"gy": (b + d) % GY}, device_id_type=MESH)
        return 0

    lax.fori_loop(1, GX, greet_x, 0)
    lax.fori_loop(1, GY, greet_y, 0)
    pl.semaphore_wait(barrier, GX + GY - 2)

    def far_first(step, size):
        half = (step + 1) // 2
        return size // 2 + half - 2 * half * (step % 2)

    def send_y(stage, src, dst):
        def go(step, _):
            peer = (b + far_first(step, GY)) % GY
            pltpu.make_async_remote_copy(
                src.at[peer], dst.at[b], ssem.at[stage], rsem.at[stage],
                device_id={"gy": peer}, device_id_type=MESH,
            ).start()
            return 0

        lax.fori_loop(0, GY - 1, go, 0)
        dst[b] = src[b]

    def send_x(stage, src_of, dst_of):
        def go(step, _):
            peer = (a + far_first(step, GX)) % GX
            pltpu.make_async_remote_copy(
                src_of(peer), dst_of(a), ssem.at[stage], rsem.at[stage],
                device_id={"gx": peer}, device_id_type=MESH,
            ).start()
            return 0

        lax.fori_loop(0, GX - 1, go, 0)

    def wait_for(sem, like):
        pltpu.make_async_copy(like, like, sem).wait()

    for c in range(2):
        for r in range(2):
            for h in range(2):
                s1[:, c * 4 + r * 2 + h, :] = star[c * 2 + h, pl.ds(r, 16, stride=2), :]
    send_y(0, s1, r1)

    shape = (32, 256)
    m2 = lax.broadcasted_iota(jnp.int32, shape, 0)
    lane = lax.broadcasted_iota(jnp.int32, shape, 1)
    kx = 2 * b + lane // 128 + 32 * m2
    ky = a // 2 + 16 * ((a % 2) * 128 + lane % 128)
    wx = jnp.where(kx >= NX // 2, kx - NX, kx).astype(f32) * (2.0 * math.pi / NX)
    wy = jnp.where(ky >= NY // 2, ky - NY, ky).astype(f32) * (2.0 * math.pi / NY)
    den = wx * wx + wy * wy
    origin = (kx == 0) & (ky == 0)
    den = jnp.where(origin, 1.0, den)
    scale = 1.0 / (NX * NY)
    share = scale / den
    g_re = 0.5 * (wy * wy - wx * wx) * share
    g_im = -(wx * wy) * share
    g_im = jnp.where((kx == NX // 2) != (ky == NY // 2), 0.0, g_im)
    g_one = jnp.where(origin, 0.5 * scale, g_re)
    g_two = jnp.where(origin, -0.5 * scale, g_re)

    wait_for(rsem.at[0], r1.at[pl.ds(0, GY - 1)])

    tr, ti = tw[0], tw[1]
    x = jnp.concatenate(
        [
            jnp.concatenate([r1[:, c * 4 + k, :] for k in range(4)], axis=1)
            for c in range(2)
        ],
        axis=0,
    )
    y = left_product(t_a[0], x)
    lines = []
    for r in range(2):
        yr, yi = y[:16, r * 256 : r * 256 + 256], y[16:, r * 256 : r * 256 + 256]
        lines.append(jnp.concatenate([yr * tr - yi * ti, yr * ti + yi * tr], axis=1))
    o = right_product(jnp.concatenate(lines, axis=0), t_b)
    for c in range(2):
        for r in range(2):
            for h in range(2):
                at = c * 256 + h * 128
                s2[:, h, c * 2 + r, :] = o[r * 16 : r * 16 + 16, at : at + 128]
    send_x(1, lambda peer: s2.at[peer // 2, peer % 2], lambda me: r2.at[me])
    r2[a] = s2[a // 2, a % 2]
    wait_for(rsem.at[1], r2.at[pl.ds(0, GX - 1)])

    x = jnp.concatenate(
        [jnp.concatenate([r2[:, c * 2 + r, :] for r in range(2)], axis=1) for c in range(2)], axis=0
    )
    y = left_product(t_s[0], x)
    column = twr[b]
    for r in range(2):
        cr, ci = column[:, 2 * r : 2 * r + 1], column[:, 2 * r + 1 : 2 * r + 2]
        yr, yi = y[:32, r * 128 : r * 128 + 128], y[32:, r * 128 : r * 128 + 128]
        for c, value in enumerate((yr * cr - yi * ci, yr * ci + yi * cr)):
            for t in range(2):
                s3[:, c * 4 + r * 2 + t, :] = value[t * 16 : t * 16 + 16]
    send_y(2, s3, r3)
    wait_for(rsem.at[2], r3.at[pl.ds(0, GY - 1)])
    x = jnp.concatenate(
        [
            jnp.concatenate([r3[:, c * 4 + r * 2 + t, :] for t in range(2)], axis=1)
            for c in range(2)
            for r in range(2)
        ],
        axis=0,
    )
    y = left_product(t_s[2], x)
    yr, yi = y[:32], y[32:]

    q = jnp.concatenate([g_one * yr - g_im * yi, -(g_two * yi + g_im * yr)], axis=0)

    y = left_product(t_s[3], q)
    for c in range(2):
        for r in range(2):
            for t in range(2):
                row = c * 32 + r * 16
                s4[:, c * 4 + r * 2 + t, :] = y[row : row + 16, t * 128 : t * 128 + 128]
    send_y(3, s4, r4)
    wait_for(rsem.at[3], r4.at[pl.ds(0, GY - 1)])
    halves = [[], []]
    for r in range(2):
        cr, ci = column[:, 2 * r : 2 * r + 1], column[:, 2 * r + 1 : 2 * r + 2]
        yr, yi = (
            jnp.concatenate([r4[:, c * 4 + r * 2 + t, :] for t in range(2)], axis=0) for c in range(2)
        )
        halves[0].append(yr * cr - yi * ci)
        halves[1].append(yr * ci + yi * cr)
    x = jnp.concatenate([jnp.concatenate(half, axis=1) for half in halves], axis=0)
    y = left_product(t_s[1], x)
    for c in range(2):
        for r in range(2):
            s5[:, c * 2 + r, :] = y[c * 32 : c * 32 + 32, r * 128 : r * 128 + 128]
    send_x(4, lambda peer: s5.at[peer], lambda me: r5.at[me // 2, me % 2])
    r5[a // 2, a % 2] = s5[a]
    wait_for(rsem.at[4], s5.at[pl.ds(0, GX - 1)])
    x = jnp.concatenate(
        [
            jnp.concatenate([r5[:, h, c * 2 + r, :] for c in range(2) for h in range(2)], axis=1)
            for r in range(2)
        ],
        axis=0,
    )
    o = right_product(x, t_b)
    lines = [[], []]
    for r in range(2):
        yr, yi = o[r * 16 : r * 16 + 16, :256], o[r * 16 : r * 16 + 16, 256:]
        lines[0].append(yr * tr - yi * ti)
        lines[1].append(yr * ti + yi * tr)
    x = jnp.concatenate([jnp.concatenate(line, axis=1) for line in lines], axis=0)
    y = left_product(t_a[1], x)
    for c in range(2):
        for k in range(4):
            s6[:, c * 4 + k, :] = y[c * 16 : c * 16 + 16, k * 128 : k * 128 + 128]
    send_y(5, s6, r6)
    wait_for(rsem.at[5], r6.at[pl.ds(0, GY - 1)])
    for c in range(2):
        for r in range(2):
            for h in range(2):
                st[c * 2 + h, pl.ds(r, 16, stride=2), :] = r6[:, c * 4 + r * 2 + h, :]
    for c in range(2):
        for h in range(2):
            lanes = slice(h * 128, h * 128 + 128)
            out[c, :, lanes] = 0.5 * star[c * 2 + h] + st[c * 2 + h]

    for stage, buffer in ((0, s1), (2, s3), (3, s4), (5, s6)):
        wait_for(ssem.at[stage], buffer.at[pl.ds(0, GY - 1)])
    wait_for(ssem.at[1], r2.at[pl.ds(0, GX - 1)])
    wait_for(ssem.at[4], s5.at[pl.ds(0, GX - 1)])


def project(star):
    whole = pl.BlockSpec(memory_space=pltpu.VMEM)
    y_buf = pltpu.VMEM((16, 8, 128), f32)
    x_buf = pltpu.VMEM((32, 4, 128), f32)
    pair_buf = pltpu.VMEM((16, 2, 4, 128), f32)
    t_a, t_b, tw, t_s, twr = (jnp.asarray(t) for t in tables())
    return pl.pallas_call(
        spectral_kernel,
        out_shape=jax.ShapeDtypeStruct((2, 32, 256), f32),
        in_specs=[whole] * 6,
        out_specs=whole,
        scratch_shapes=[
            pltpu.VMEM((4, 32, 128), f32),
            y_buf, y_buf, pair_buf, x_buf, y_buf, y_buf, y_buf, y_buf, x_buf, pair_buf, y_buf, y_buf,
            pltpu.SemaphoreType.DMA((6,)),
            pltpu.SemaphoreType.DMA((6,)),
        ],
        compiler_params=pltpu.CompilerParams(collective_id=0, has_side_effects=True),
        name="spectral",
    )(star, t_a, t_b, tw, t_s, twr)


def on_device(u_field, v_field, w_first, b_first, w_second, b_second, w_third, b_third):
    layers = (w_first, b_first, w_second, b_second, w_third, b_third)
    star = star_fields(u_field, v_field, layers)
    result = project(star)
    return result[0], result[1]


def solution(mesh):
    return jax.shard_map(
        on_device,
        mesh=mesh,
        in_specs=(P("gx", "gy"), P("gx", "gy"), P(), P(), P(), P(), P(), P()),
        out_specs=(P("gx", "gy"), P("gx", "gy")),
        check_vma=False,
    )
```

```python
import functools
import math

import jax
import jax.numpy as jnp
import ml_dtypes
import numpy as np
from jax import lax
from jax.experimental import pallas as pl
from jax.experimental.pallas import tpu as pltpu
from jax.sharding import PartitionSpec as P

step_ratio = 0.4
stencil_base = (-0.0625, 0.5625, 0.5625, -0.0625)
GX = 32
GY = 16
NX = 1024
NY = 4096
PITCH = 272
SHIFTS = (4, 3, 2, 1, 0, -1)
MESH = pl.DeviceIdType.MESH
f32 = jnp.float32
bf16 = jnp.bfloat16


def split_bf16(table):
    hi = table.astype(np.float32).astype(ml_dtypes.bfloat16)
    lo = (table - hi.astype(np.float64)).astype(np.float32).astype(ml_dtypes.bfloat16)
    return hi, lo


def real_left(matrix):
    return np.block([[matrix.real, -matrix.imag], [matrix.imag, matrix.real]])


def triple_left(table):
    hi, lo = split_bf16(table)
    return np.concatenate([hi, hi, lo], axis=1)


def root(product, whole):
    return np.exp(-2j * np.pi * (product % whole) / whole)


@functools.cache
def tables():
    n8, n16, n32, n256 = (np.arange(n) for n in (8, 16, 32, 256))
    paired = np.concatenate([4 * n8 + t for t in range(4)])
    sign = np.concatenate([np.ones(16), -np.ones(16)])
    halves = [n8, n8 + 8]
    t_a = np.stack([triple_left(real_left(root(np.outer(k, n16), 16)) * sign[None, :]) for k in halves])
    t_a2 = np.stack([triple_left(real_left(root(np.outer(n16, k), 16)) * sign[:, None]) for k in halves])
    mid = root(np.outer(n256, n256), 256)
    t_b = np.stack(split_bf16(np.block([[mid.real, mid.imag], [-mid.imag, mid.real]])))
    turn = [root(np.outer(k, n256), 4096) for k in halves]
    tw = np.stack([np.stack([w.real, w.imag]) for w in turn]).astype(np.float32)
    t_s = np.stack(
        [
            triple_left(real_left(root(np.outer(paired, n32), 32))),
            triple_left(real_left(root(np.outer(n32, paired), 32))),
        ]
    )
    twr = np.zeros((8, 32, 8), np.float32)
    for r in range(4):
        row = root(np.outer(4 * n8 + r, paired), 1024)
        twr[:, :, 2 * r] = row.real
        twr[:, :, 2 * r + 1] = row.imag
    return t_a, t_a2, t_b, tw, t_s, twr


def triple(value):
    hi = value.astype(bf16)
    lo = (value - hi.astype(f32)).astype(bf16)
    return jnp.concatenate([hi, lo, hi], axis=0)


def left_product(table, value):
    return jnp.dot(table, triple(value), preferred_element_type=f32)


def right_product(value, t_b):
    rows = value.shape[0]
    hi = value.astype(bf16)
    lo = (value - hi.astype(f32)).astype(bf16)
    both = jnp.dot(jnp.concatenate([hi, lo], axis=0), t_b[0], preferred_element_type=f32)
    return both[:rows] + both[rows:] + jnp.dot(hi, t_b[1], preferred_element_type=f32)


def nt(left, right):
    return lax.dot_general(left, right, (((1,), (1,)), ((), ())), preferred_element_type=f32)


def swap_halves(low, high, lane):
    first = lane < 64
    return jnp.where(first, low, pltpu.roll(high, 64, 1)), jnp.where(first, pltpu.roll(low, 64, 1), high)


def far_first(step, size):
    half = (step + 1) // 2
    return size // 2 + half - 2 * half * (step % 2)


def wait_for(sem, like):
    pltpu.make_async_copy(like, like, sem).wait()


def kernel(names, *refs):
    r = dict(zip(names, refs))
    a = lax.axis_index("gx")
    b = lax.axis_index("gy")
    y_at, x_hi = b // 2, b % 2

    local = []
    for n, name in enumerate(("u", "v", "w1", "w2", "w3", "b1", "b2", "b3", "t_a", "t_a2", "t_b", "tw", "t_s", "twr")):
        copy = pltpu.make_async_copy(r[name + "_hbm"], r[name], r["lsem"].at[n])
        copy.start()
        local.append(copy)
    u, v = r["u"], r["v"]

    moves = [(dx, dy) for dx in (-1, 0, 1) for dy in (-1, 0, 1) if (dx, dy) != (0, 0)]

    def at(dx, dy):
        return {"gx": (a + dx + GX) % GX, "gy": (b + dy + GY) % GY}

    barrier = pltpu.get_barrier_semaphore()
    for dx, dy in moves:
        if dx and dy:
            pl.semaphore_signal(barrier, inc=1, device_id=at(dx, dy), device_id_type=MESH)

    def greet_y(step, _):
        peer = (b + far_first(step, GY)) % GY
        pl.semaphore_signal(barrier, inc=1, device_id={"gy": peer}, device_id_type=MESH)
        return 0

    def greet_x(step, _):
        peer = (a + far_first(step, GX)) % GX
        pl.semaphore_signal(barrier, inc=1, device_id={"gx": peer}, device_id_type=MESH)
        return 0

    lax.fori_loop(0, GY - 1, greet_y, 0)
    lax.fori_loop(0, GX - 1, greet_x, 0)
    local[0].wait()
    local[1].wait()
    pl.semaphore_wait(barrier, GX + GY + 2)

    copies = []
    for n, (dx, dy) in enumerate(moves):
        rows = {-1: slice(0, 8), 0: slice(0, 32), 1: slice(24, 32)}[dx]
        cols = {-1: slice(0, 128), 0: slice(0, 256), 1: slice(128, 256)}[dy]
        for c, field in enumerate((u, v)):
            if dx and dy:
                dst = r["corner_in"].at[(dx + 1) // 2, (dy + 1) // 2, c]
            elif dx:
                dst = r["rows_in"].at[(dx + 1) // 2, c]
            else:
                dst = r["cols_in"].at[(dy + 1) // 2, c]
            copy = pltpu.make_async_remote_copy(
                field.at[rows, cols], dst, r["hssem"].at[2 * n + c], r["hrsem"].at[2 * n + c],
                device_id=at(dx, dy), device_id_type=MESH,
            )
            copy.start()
            copies.append(copy)

    k1, k2, k3, x1, x2, fs, cf = (r[n] for n in ("k1", "k2", "k3", "x1", "x2", "fs", "cf"))
    k1[...] = jnp.zeros_like(k1)
    k2[...] = jnp.zeros_like(k2)
    k3[...] = jnp.zeros_like(k3)
    for copy in local[2:]:
        copy.wait()
    w1, w2, w3, b3 = (r[n] for n in ("w1", "w2", "w3", "b3"))
    for dj in range(3):
        for dr in range(3):
            tap = 3 * dr + dj
            for o in range(5):
                x = o + dr
                row = dj * 80 + o * 16
                k3[row : row + 16, x * 64 : x * 64 + 64] = w3[tap]
                if o == 4:
                    continue
                for c in range(2):
                    row = (dj * 2 + c) * 8 + x
                    k1[row : row + 1, o * 64 : o * 64 + 64] = w1[tap, c : c + 1, :].astype(f32)
                k2[dj, o * 64 : o * 64 + 64, x * 64 : x * 64 + 64] = w2[tap]
    bias1 = jnp.concatenate([r["b1"][...]] * 4, axis=1)
    bias2 = jnp.concatenate([r["b2"][...]] * 4, axis=1)
    x1[:, pl.ds(10 * PITCH, 16), :] = jnp.zeros((2, 16, 128), f32)
    x2[pl.ds(9 * PITCH, 384), :] = jnp.zeros((384, 256), bf16)

    shape = (32, 256)
    m2 = lax.broadcasted_iota(jnp.int32, shape, 0)
    lane = lax.broadcasted_iota(jnp.int32, shape, 1)
    kx = 4 * y_at + lane // 64 + 32 * m2
    ky = a // 4 + 8 * x_hi + 16 * ((a % 4) * 64 + lane % 64)
    wx = jnp.where(kx >= NX // 2, kx - NX, kx).astype(f32) * (2.0 * math.pi / NX)
    wy = jnp.where(ky >= NY // 2, ky - NY, ky).astype(f32) * (2.0 * math.pi / NY)
    den = wx * wx + wy * wy
    origin = (kx == 0) & (ky == 0)
    den = jnp.where(origin, 1.0, den)
    scale = 1.0 / (NX * NY)
    share = scale / den
    g_re = 0.5 * (wy * wy - wx * wx) * share
    g_im = jnp.where((kx == NX // 2) != (ky == NY // 2), 0.0, -(wx * wy) * share)
    r["gain"][0] = jnp.where(origin, 0.5 * scale, g_re)
    r["gain"][1] = jnp.where(origin, -0.5 * scale, g_re)
    r["gain"][2] = g_im

    for copy in copies:
        copy.wait_recv()

    lane = lax.broadcasted_iota(jnp.int32, (8, 128), 1)
    for c, field in enumerate((u, v)):
        for g in range(6):
            if g in (0, 5):
                e = 1 if g == 0 else 0
                corner, rows_in = r["corner_in"], r["rows_in"]
                tiles = [corner[e, 1, c], rows_in[e, c, :, 0:128], rows_in[e, c, :, 128:256], corner[e, 0, c]]
            else:
                rows = slice(g * 8 - 8, g * 8)
                cols_in = r["cols_in"]
                tiles = [cols_in[1, c, rows, :], field[rows, 0:128], field[rows, 128:256], cols_in[0, c, rows, :]]
            for n, s in enumerate(SHIFTS):
                turned = [pltpu.roll(tile, s % 128, 1) if s else tile for tile in tiles]
                for k in range(3):
                    if s > 0:
                        value = jnp.where(lane < s, turned[k], turned[k + 1])
                    elif s < 0 and k < 2:
                        value = jnp.where(lane >= 128 + s, turned[k + 2], turned[k + 1])
                    else:
                        value = turned[k + 1]
                    fs[n, c, k, g * 8 : g * 8 + 8, :] = value

    first_weights = k1[...].astype(bf16)

    def layer_1(i, _):
        patch = jnp.concatenate(
            [
                jnp.concatenate([fs[dj, c, k, pl.ds(4 * i + 4, 8), :] for k in range(3)], axis=1)
                for dj in range(3)
                for c in range(2)
            ],
            axis=0,
        ).astype(bf16)
        y = lax.dot_general(patch, first_weights, (((0,), (0,)), ((), ())), preferred_element_type=f32)
        y = jnp.maximum(y[:PITCH] + bias1, 0.0)
        start = pl.multiple_of(i * PITCH, 8)
        x1[0, pl.ds(start, PITCH), :] = y[:, :128]
        x1[1, pl.ds(start, PITCH), :] = y[:, 128:]
        return 0

    lax.fori_loop(0, 10, layer_1, 0)

    chunk = 3 * PITCH

    def layer_2(i, _):
        start = i * chunk

        def piece(half, offset):
            return x1[half, pl.ds(start + offset, chunk), :].astype(bf16)

        y = None
        for dj in range(3):
            left = jnp.concatenate([piece(0, dj), piece(1, dj)], axis=1)
            term = nt(left, k2[dj, :, 0:256])
            y = term if y is None else y + term
        left = jnp.concatenate([piece(0, PITCH), piece(0, PITCH + 1)], axis=1)
        y = y + nt(left, jnp.concatenate([k2[0, :, 256:384], k2[1, :, 256:384]], axis=1))
        y = y + nt(piece(0, PITCH + 2), k2[2, :, 256:384])
        x2[pl.ds(pl.multiple_of(start, 16), chunk), :] = jnp.maximum(y + bias2, 0.0).astype(bf16)
        return 0

    lax.fori_loop(0, 3, layer_2, 0)

    s1, r1, st = r["s1"], r["r1"], r["st"]
    ssem, rsem = r["ssem"], r["rsem"]

    def layer_3(step, _):
        i = (y_at + far_first(step, 8)) % 8
        start = pl.multiple_of(i * PITCH, 16)
        after = pl.multiple_of((i + 1) * PITCH, 16)
        y = nt(k3[:, 0:256], x2[pl.ds(start, 384), :]) + nt(k3[:, 256:448], x2[pl.ds(after, 384), 0:192])
        y = y[0:80] + pltpu.roll(y[80:160], 383, 1) + pltpu.roll(y[160:240], 382, 1)
        for o in range(5):
            for k in range(3):
                cf[k, pl.ds(o, 16, stride=8), :] = y[o * 16 : o * 16 + 16, k * 128 : k * 128 + 128]

        def field_at(c, s, down, k):
            return fs[SHIFTS.index(s), c, k, pl.ds(4 * i + 7 + down, 8), :]

        flows = [[[], []] for _ in range(2)]
        for k in range(3):
            carry = (
                0.5 * (field_at(0, 1, 0, k) + field_at(0, 1, 1, k)),
                0.5 * (field_at(1, 1, 0, k) + field_at(1, 0, 0, k)),
            )
            for q in range(2):
                for d in range(2):
                    if d == 0:
                        taps = [field_at(q, 1, down, k) for down in (-1, 0, 1, 2)]
                    else:
                        taps = [field_at(q, s, 0, k) for s in (2, 1, 0, -1)]
                    base = 8 * d + 4 * q
                    weights = [cf[k, (base + s) * 8 : (base + s) * 8 + 8, :] + b3[base + s] for s in range(4)]
                    mean = 0.25 * ((weights[0] + weights[1]) + (weights[2] + weights[3]))
                    total = None
                    for s in range(4):
                        term = (stencil_base[s] + weights[s] - mean) * taps[s]
                        total = term if total is None else total + term
                    flows[d][q].append(carry[d] * total)
        for q in range(2):
            along_x = jnp.concatenate(flows[0][q], axis=1)
            along_y = jnp.concatenate(flows[1][q], axis=1)
            change = pltpu.roll(along_x + (along_y - pltpu.roll(along_y, 1, 1)), 7, 0) - along_x
            here = jnp.concatenate([field_at(q, 1, 1, k) for k in range(3)], axis=1)
            moved = pltpu.roll(here - step_ratio * change, 383, 1)
            for h in range(2):
                value = moved[0:4, h * 128 : h * 128 + 128]
                st[q * 2 + h, pl.ds(4 * i, 4), :] = value
                s1[i, q * 8 + h * 4 : q * 8 + h * 4 + 4, :] = value
        for other in range(2):
            peer = 2 * i + other

            @pl.when(peer != b)
            def _():
                pltpu.make_async_remote_copy(
                    s1.at[i], r1.at[b], ssem.at[0], rsem.at[0], device_id={"gy": peer}, device_id_type=MESH
                ).start()

        return 0

    lax.fori_loop(0, 8, layer_3, 0)
    r1[b] = s1[y_at]

    def send(stage, axis, size, peer_of, src_of, dst):
        def go(step, _):
            peer = peer_of(step)
            pltpu.make_async_remote_copy(
                src_of(peer), dst, ssem.at[stage], rsem.at[stage], device_id={axis: peer}, device_id_type=MESH
            ).start()
            return 0

        lax.fori_loop(0, size - 1, go, 0)

    def x_peer(step):
        return (a + far_first(step, GX)) % GX

    def y_peer(step):
        return 2 * ((y_at + far_first(step, 8)) % 8) + x_hi

    def all_y_peer(step):
        return (b + far_first(step, GY)) % GY

    wait_for(rsem.at[0], r1.at[pl.ds(0, GY - 1)])

    tr, ti = r["tw"][x_hi, 0], r["tw"][x_hi, 1]
    x = jnp.concatenate(
        [
            jnp.concatenate([r1[:, c * 8 + h * 4 + i, :] for i in range(4) for h in range(2)], axis=1)
            for c in range(2)
        ],
        axis=0,
    )
    y = left_product(r["t_a"][x_hi], x)
    lines = []
    for i in range(4):
        yr, yi = y[:8, i * 256 : i * 256 + 256], y[8:, i * 256 : i * 256 + 256]
        lines.append(jnp.concatenate([yr * tr - yi * ti, yr * ti + yi * tr], axis=1))
    o = right_product(jnp.concatenate(lines, axis=0), r["t_b"])
    s2, r2 = r["s2"], r["r2"]
    for c in range(2):
        for rp in range(2):
            for h in range(2):
                cols = slice(c * 256 + h * 128, c * 256 + h * 128 + 128)
                pair = swap_halves(o[rp * 16 : rp * 16 + 8, cols], o[rp * 16 + 8 : rp * 16 + 16, cols], lane)
                for low in range(2):
                    s2[:, 2 * h + low, c * 2 + rp, :] = pair[low]
    send(1, "gx", GX, x_peer, lambda peer: s2.at[peer // 4, peer % 4], r2.at[a])
    r2[a] = s2[a // 4, a % 4]
    wait_for(rsem.at[1], r2.at[pl.ds(0, GX - 1)])

    x = jnp.concatenate(
        [jnp.concatenate([r2[:, c * 2 + rp, :] for rp in range(2)], axis=1) for c in range(2)], axis=0
    )
    y = left_product(r["t_s"][0], x)
    column = r["twr"][y_at]
    wide = lax.broadcasted_iota(jnp.int32, (32, 128), 1) < 64
    turns = [
        [jnp.where(wide, column[:, 4 * rp + c : 4 * rp + c + 1], column[:, 4 * rp + 2 + c : 4 * rp + 3 + c]) for c in range(2)]
        for rp in range(2)
    ]
    s3, r3 = r["s3"], r["r3"]
    for rp in range(2):
        cr, ci = turns[rp]
        yr, yi = y[:32, rp * 128 : rp * 128 + 128], y[32:, rp * 128 : rp * 128 + 128]
        for c, value in enumerate((yr * cr - yi * ci, yr * ci + yi * cr)):
            for tp in range(2):
                pair = swap_halves(value[tp * 16 : tp * 16 + 8], value[tp * 16 + 8 : tp * 16 + 16], lane)
                for low in range(2):
                    s3[:, c * 8 + (2 * rp + low) * 2 + tp, :] = pair[low]
    send(2, "gy", 8, y_peer, lambda peer: s3.at[peer // 2], r3.at[y_at])
    r3[y_at] = s3[y_at]
    wait_for(rsem.at[2], r3.at[pl.ds(0, 7)])
    x = jnp.concatenate(
        [
            jnp.concatenate([r3[:, c * 8 + i * 2 + tp, :] for tp in range(2)], axis=1)
            for c in range(2)
            for i in range(4)
        ],
        axis=0,
    )
    y = left_product(r["t_s"][1], x)
    yr, yi = y[:32], y[32:]

    gain = r["gain"]
    q = jnp.concatenate([gain[0] * yr - gain[2] * yi, -(gain[1] * yi + gain[2] * yr)], axis=0)

    y = left_product(r["t_s"][0], q)
    s4, r4 = r["s4"], r["r4"]
    for c in range(2):
        for i in range(4):
            for tp in range(2):
                row = c * 32 + i * 8
                s4[:, c * 8 + i * 2 + tp, :] = y[row : row + 8, tp * 128 : tp * 128 + 128]
    send(3, "gy", 8, y_peer, lambda peer: s4.at[peer // 2], r4.at[y_at])
    r4[y_at] = s4[y_at]
    wait_for(rsem.at[3], r4.at[pl.ds(0, 7)])
    halves = [[], []]
    for rp in range(2):
        cr, ci = turns[rp]
        parts = []
        for c in range(2):
            rows = []
            for tp in range(2):
                rows += swap_halves(r4[:, c * 8 + 4 * rp + tp, :], r4[:, c * 8 + 4 * rp + 2 + tp, :], lane)
            parts.append(jnp.concatenate(rows, axis=0))
        yr, yi = parts
        halves[0].append(yr * cr - yi * ci)
        halves[1].append(yr * ci + yi * cr)
    x = jnp.concatenate([jnp.concatenate(half, axis=1) for half in halves], axis=0)
    y = left_product(r["t_s"][1], x)
    s5, r5 = r["s5"], r["r5"]
    for c in range(2):
        for rp in range(2):
            s5[:, c * 2 + rp, :] = y[c * 32 : c * 32 + 32, rp * 128 : rp * 128 + 128]
    send(4, "gx", GX, x_peer, lambda peer: s5.at[peer], r5.at[a // 4, a % 4])
    r5[a // 4, a % 4] = s5[a]
    wait_for(rsem.at[4], s5.at[pl.ds(0, GX - 1)])
    lines = [[None] * 4 for _ in range(4)]
    for c in range(2):
        for rp in range(2):
            for h in range(2):
                pair = swap_halves(r5[:, 2 * h, c * 2 + rp, :], r5[:, 2 * h + 1, c * 2 + rp, :], lane)
                for low in range(2):
                    lines[2 * rp + low][c * 2 + h] = pair[low]
    x = jnp.concatenate([jnp.concatenate(line, axis=1) for line in lines], axis=0)
    o = right_product(x, r["t_b"])
    lines = [[], []]
    for i in range(4):
        yr, yi = o[i * 8 : i * 8 + 8, :256], o[i * 8 : i * 8 + 8, 256:]
        lines[0].append(yr * tr - yi * ti)
        lines[1].append(yr * ti + yi * tr)
    x = jnp.concatenate([jnp.concatenate(line, axis=1) for line in lines], axis=0)
    y = left_product(r["t_a2"][x_hi], x)
    s6, r6 = r["s6"], r["r6"]
    for c in range(2):
        for i in range(4):
            for h in range(2):
                at_lane = i * 256 + h * 128
                s6[:, c * 8 + h * 4 + i, :] = y[c * 16 : c * 16 + 16, at_lane : at_lane + 128]
    send(5, "gy", GY, all_y_peer, lambda peer: s6.at[peer], r6.at[y_at, x_hi])
    r6[y_at, x_hi] = s6[b]
    wait_for(rsem.at[5], s6.at[pl.ds(0, GY - 1)])
    back = r["back"]
    for c, out in enumerate((r["u_next"], r["v_next"])):
        for h in range(2):
            for i in range(4):
                index = c * 8 + h * 4 + i
                back[pl.ds(i, 8, stride=4), :] = r6[:, 0, index, :] + r6[:, 1, index, :]
            out[:, h * 128 : h * 128 + 128] = 0.5 * st[c * 2 + h] + back[...]

    for copy in copies:
        copy.wait_send()
    for stage, like in (
        (0, r1.at[pl.ds(0, GY - 1)]),
        (1, r2.at[pl.ds(0, GX - 1)]),
        (2, s3.at[pl.ds(0, 7)]),
        (3, s4.at[pl.ds(0, 7)]),
        (4, s5.at[pl.ds(0, GX - 1)]),
        (5, s6.at[pl.ds(0, GY - 1)]),
    ):
        wait_for(ssem.at[stage], like)


def on_device(u_field, v_field, w_first, b_first, w_second, b_second, w_third, b_third):
    inputs = {
        "u": u_field, "v": v_field, "w1": jnp.transpose(w_first, (0, 2, 1)), "w2": w_second, "w3": w_third,
        "b1": b_first[None], "b2": b_second[None], "b3": b_third,
    }
    inputs.update(zip(("t_a", "t_a2", "t_b", "tw", "t_s", "twr"), (jnp.asarray(t) for t in tables())))
    scratch = {
        name: (pltpu.SMEM if name == "b3" else pltpu.VMEM)(value.shape, value.dtype)
        for name, value in inputs.items()
    }
    scratch |= {
        "rows_in": pltpu.VMEM((2, 2, 8, 256), f32),
        "cols_in": pltpu.VMEM((2, 2, 32, 128), f32),
        "corner_in": pltpu.VMEM((2, 2, 2, 8, 128), f32),
        "fs": pltpu.VMEM((6, 2, 3, 56, 128), f32),
        "k1": pltpu.VMEM((48, 256), f32),
        "k2": pltpu.VMEM((3, 256, 384), bf16),
        "k3": pltpu.VMEM((240, 512), bf16),
        "x1": pltpu.VMEM((2, 10 * PITCH + 16, 128), f32),
        "x2": pltpu.VMEM((9 * PITCH + 384, 256), bf16),
        "cf": pltpu.VMEM((3, 128, 128), f32),
        "st": pltpu.VMEM((4, 32, 128), f32),
        "back": pltpu.VMEM((32, 128), f32),
        "gain": pltpu.VMEM((3, 32, 256), f32),
        "s1": pltpu.VMEM((8, 16, 128), f32),
        "r1": pltpu.VMEM((16, 16, 128), f32),
        "s2": pltpu.VMEM((8, 4, 4, 128), f32),
        "r2": pltpu.VMEM((32, 4, 128), f32),
        "s3": pltpu.VMEM((8, 16, 128), f32),
        "r3": pltpu.VMEM((8, 16, 128), f32),
        "s4": pltpu.VMEM((8, 16, 128), f32),
        "r4": pltpu.VMEM((8, 16, 128), f32),
        "s5": pltpu.VMEM((32, 4, 128), f32),
        "r5": pltpu.VMEM((8, 4, 4, 128), f32),
        "s6": pltpu.VMEM((16, 16, 128), f32),
        "r6": pltpu.VMEM((8, 2, 16, 128), f32),
        "lsem": pltpu.SemaphoreType.DMA((len(inputs),)),
        "hssem": pltpu.SemaphoreType.DMA((16,)),
        "hrsem": pltpu.SemaphoreType.DMA((16,)),
        "ssem": pltpu.SemaphoreType.DMA((6,)),
        "rsem": pltpu.SemaphoreType.DMA((6,)),
    }
    names = [name + "_hbm" for name in inputs] + ["u_next", "v_next"] + list(scratch)
    block = jax.ShapeDtypeStruct((32, 256), f32)
    return pl.pallas_call(
        functools.partial(kernel, names),
        out_shape=(block, block),
        in_specs=[pl.BlockSpec(memory_space=pltpu.HBM)] * len(inputs),
        out_specs=(pl.BlockSpec(memory_space=pltpu.VMEM),) * 2,
        scratch_shapes=list(scratch.values()),
        compiler_params=pltpu.CompilerParams(collective_id=0, has_side_effects=True),
        name="step",
    )(*inputs.values())


def solution(mesh):
    return jax.shard_map(
        on_device,
        mesh=mesh,
        in_specs=(P("gx", "gy"), P("gx", "gy"), P(), P(), P(), P(), P(), P()),
        out_specs=(P("gx", "gy"), P("gx", "gy")),
        check_vma=False,
    )
```

```python
import functools
import math

import jax
import jax.numpy as jnp
import ml_dtypes
import numpy as np
from jax import lax
from jax.experimental import pallas as pl
from jax.experimental.pallas import tpu as pltpu
from jax.sharding import PartitionSpec as P

step_ratio = 0.4
stencil_base = (-0.0625, 0.5625, 0.5625, -0.0625)
GX = 32
GY = 16
NX = 1024
NY = 4096
PITCH = 272
SHIFTS = (4, 3, 2, 1, 0, -1)
MESH = pl.DeviceIdType.MESH
f32 = jnp.float32
bf16 = jnp.bfloat16


def split_bf16(table):
    hi = table.astype(np.float32).astype(ml_dtypes.bfloat16)
    lo = (table - hi.astype(np.float64)).astype(np.float32).astype(ml_dtypes.bfloat16)
    return hi, lo


def real_left(matrix):
    return np.block([[matrix.real, -matrix.imag], [matrix.imag, matrix.real]])


def triple_left(table):
    hi, lo = split_bf16(table)
    return np.concatenate([hi, hi, lo], axis=1)


def root(product, whole):
    return np.exp(-2j * np.pi * (product % whole) / whole)


@functools.cache
def tables():
    n8, n16, n32, n256 = (np.arange(n) for n in (8, 16, 32, 256))
    paired = np.concatenate([4 * n8 + t for t in range(4)])
    sign = np.concatenate([np.ones(16), -np.ones(16)])
    halves = [n8, n8 + 8]
    t_a = np.stack([triple_left(real_left(root(np.outer(k, n16), 16)) * sign[None, :]) for k in halves])
    t_a2 = np.stack([triple_left(real_left(root(np.outer(n16, k), 16)) * sign[:, None]) for k in halves])
    mid = root(np.outer(n256, n256), 256)
    t_b = np.stack(split_bf16(np.block([[mid.real, mid.imag], [-mid.imag, mid.real]])))
    turn = [root(np.outer(k, n256), 4096) for k in halves]
    tw = np.stack([np.stack([w.real, w.imag]) for w in turn]).astype(np.float32)
    t_s = np.stack(
        [
            triple_left(real_left(root(np.outer(paired, n32), 32))),
            triple_left(real_left(root(np.outer(n32, paired), 32))),
        ]
    )
    twr = np.zeros((8, 32, 8), np.float32)
    for r in range(4):
        row = root(np.outer(4 * n8 + r, paired), 1024)
        twr[:, :, 2 * r] = row.real
        twr[:, :, 2 * r + 1] = row.imag
    return t_a, t_a2, t_b, tw, t_s, twr


def triple(value):
    hi = value.astype(bf16)
    lo = (value - hi.astype(f32)).astype(bf16)
    return jnp.concatenate([hi, lo, hi], axis=0)


def left_product(table, value):
    return jnp.dot(table, triple(value), preferred_element_type=f32)


def right_product(value, t_b):
    rows = value.shape[0]
    hi = value.astype(bf16)
    lo = (value - hi.astype(f32)).astype(bf16)
    both = jnp.dot(jnp.concatenate([hi, lo], axis=0), t_b[0], preferred_element_type=f32)
    return both[:rows] + both[rows:] + jnp.dot(hi, t_b[1], preferred_element_type=f32)


def nt(left, right):
    return lax.dot_general(left, right, (((1,), (1,)), ((), ())), preferred_element_type=f32)


def swap_halves(low, high, lane):
    first = lane < 64
    return jnp.where(first, low, pltpu.roll(high, 64, 1)), jnp.where(first, pltpu.roll(low, 64, 1), high)


def far_first(step, size):
    half = (step + 1) // 2
    return size // 2 + half - 2 * half * (step % 2)


def wait_for(sem, like):
    pltpu.make_async_copy(like, like, sem).wait()


def kernel(names, *refs):
    r = dict(zip(names, refs))
    a = lax.axis_index("gx")
    b = lax.axis_index("gy")
    y_at, x_hi = b // 2, b % 2

    local = []
    for n, name in enumerate(("u", "v", "w1", "w2", "w3", "b1", "b2", "b3", "t_a", "t_a2", "t_b", "tw", "t_s", "twr")):
        copy = pltpu.make_async_copy(r[name + "_hbm"], r[name], r["lsem"].at[n])
        copy.start()
        local.append(copy)
    u, v = r["u"], r["v"]

    moves = [(dx, dy) for dx in (-1, 0, 1) for dy in (-1, 0, 1) if (dx, dy) != (0, 0)]

    def at(dx, dy):
        return {"gx": (a + dx + GX) % GX, "gy": (b + dy + GY) % GY}

    barrier = pltpu.get_barrier_semaphore()
    for dx, dy in moves:
        if dx and dy:
            pl.semaphore_signal(barrier, inc=1, device_id=at(dx, dy), device_id_type=MESH)

    def greet_y(step, _):
        peer = (b + far_first(step, GY)) % GY
        pl.semaphore_signal(barrier, inc=1, device_id={"gy": peer}, device_id_type=MESH)
        return 0

    def greet_x(step, _):
        peer = (a + far_first(step, GX)) % GX
        pl.semaphore_signal(barrier, inc=1, device_id={"gx": peer}, device_id_type=MESH)
        return 0

    lax.fori_loop(0, GY - 1, greet_y, 0)
    lax.fori_loop(0, GX - 1, greet_x, 0)
    k1, k2, k3, x1, x2, fs, cf = (r[n] for n in ("k1", "k2", "k3", "x1", "x2", "fs", "cf"))
    k1[...] = jnp.zeros_like(k1)
    k2[...] = jnp.zeros_like(k2)
    k3[...] = jnp.zeros_like(k3)
    for copy in local:
        copy.wait()
    w1, w2, w3, b3 = (r[n] for n in ("w1", "w2", "w3", "b3"))
    for dj in range(3):
        for dr in range(3):
            tap = 3 * dr + dj
            for o in range(5):
                x = o + dr
                row = dj * 80 + o * 16
                k3[row : row + 16, x * 64 : x * 64 + 64] = w3[tap]
                if o == 4:
                    continue
                for c in range(2):
                    row = (dj * 2 + c) * 8 + x
                    k1[row : row + 1, o * 64 : o * 64 + 64] = w1[tap, c : c + 1, :].astype(f32)
                k2[dj, o * 64 : o * 64 + 64, x * 64 : x * 64 + 64] = w2[tap]
    bias1 = jnp.concatenate([r["b1"][...]] * 4, axis=1)
    bias2 = jnp.concatenate([r["b2"][...]] * 4, axis=1)
    x1[:, pl.ds(10 * PITCH, 16), :] = jnp.zeros((2, 16, 128), f32)
    x2[pl.ds(9 * PITCH, 384), :] = jnp.zeros((384, 256), bf16)

    lane = lax.broadcasted_iota(jnp.int32, (8, 128), 1)

    def surround(groups, arrived):
        for c, field in enumerate((u, v)):
            for g in groups:
                if g in (0, 5):
                    e = 1 if g == 0 else 0
                    corner, rows_in = r["corner_in"], r["rows_in"]
                    tiles = [corner[e, 1, c], rows_in[e, c, :, 0:128], rows_in[e, c, :, 128:256], corner[e, 0, c]]
                else:
                    rows = slice(g * 8 - 8, g * 8)
                    tiles = [field[rows, 0:128], field[rows, 128:256]]
                    if arrived:
                        cols_in = r["cols_in"]
                        tiles = [cols_in[1, c, rows, :], *tiles, cols_in[0, c, rows, :]]
                    else:
                        tiles = [tiles[1], *tiles, tiles[0]]
                for n, s in enumerate(SHIFTS):
                    turned = [pltpu.roll(tile, s % 128, 1) if s else tile for tile in tiles]
                    for k in range(3):
                        if s > 0:
                            value = jnp.where(lane < s, turned[k], turned[k + 1])
                        elif s < 0 and k < 2:
                            value = jnp.where(lane >= 128 + s, turned[k + 2], turned[k + 1])
                        else:
                            value = turned[k + 1]
                        fs[n, c, k, g * 8 : g * 8 + 8, :] = value

    first_weights = k1[...].astype(bf16)

    def patches(i, tiles):
        return [
            jnp.concatenate([fs[dj, c, k, pl.ds(4 * i + 4, 8), :] for k in tiles], axis=1)
            for dj in range(3)
            for c in range(2)
        ]

    def first(patch):
        y = lax.dot_general(
            patch.astype(bf16), first_weights, (((0,), (0,)), ((), ())), preferred_element_type=f32
        )
        return y

    def layer_1(i):
        y = first(jnp.concatenate(patches(i, range(3)), axis=0))
        y = jnp.maximum(y[:PITCH] + bias1, 0.0)
        x1[0, pl.ds(i * PITCH, PITCH), :] = y[:, :128]
        x1[1, pl.ds(i * PITCH, PITCH), :] = y[:, 128:]

    def layer_1_ends(blocks):
        wide = lax.broadcasted_iota(jnp.int32, (48, 128), 1) // 8
        slots = [(i, end) for i in blocks for end in range(2)]
        packed = jnp.zeros((48, 128), f32)
        for n, (i, end) in enumerate(slots):
            patch = jnp.concatenate(patches(i, [2 * end]), axis=0)
            packed = jnp.where(wide == n, pltpu.roll(patch, 8 * n, 1) if n else patch, packed)
        y = jnp.maximum(first(packed) + bias1, 0.0)
        for n, (i, end) in enumerate(slots):
            at_row = i * PITCH + 256 * end
            x1[0, pl.ds(at_row, 8), :] = y[8 * n : 8 * n + 8, :128]
            x1[1, pl.ds(at_row, 8), :] = y[8 * n : 8 * n + 8, 128:]

    def layer_2(stretches):
        def piece(half, offset):
            return jnp.concatenate(
                [x1[half, pl.ds(start + offset, length), :].astype(bf16) for start, length in stretches], axis=0
            )

        y = None
        for dj in range(3):
            left = jnp.concatenate([piece(0, dj), piece(1, dj)], axis=1)
            term = nt(left, k2[dj, :, 0:256])
            y = term if y is None else y + term
        left = jnp.concatenate([piece(0, PITCH), piece(0, PITCH + 1)], axis=1)
        y = y + nt(left, jnp.concatenate([k2[0, :, 256:384], k2[1, :, 256:384]], axis=1))
        y = y + nt(piece(0, PITCH + 2), k2[2, :, 256:384])
        y = jnp.maximum(y + bias2, 0.0).astype(bf16)
        row = 0
        for start, length in stretches:
            x2[pl.ds(start, length), :] = y[row : row + length]
            row += length

    surround(range(1, 5), False)
    for i in range(1, 8):
        layer_1(i)

    def inner(i, _):
        layer_2([(pl.multiple_of((3 * i + 1) * PITCH, 16), 3 * PITCH)])
        return 0

    lax.fori_loop(0, 2, inner, 0)

    pl.semaphore_wait(barrier, GX + GY + 2)

    copies = []
    for n, (dx, dy) in enumerate(moves):
        rows = {-1: slice(0, 8), 0: slice(0, 32), 1: slice(24, 32)}[dx]
        cols = {-1: slice(0, 128), 0: slice(0, 256), 1: slice(128, 256)}[dy]
        for c, field in enumerate((u, v)):
            if dx and dy:
                dst = r["corner_in"].at[(dx + 1) // 2, (dy + 1) // 2, c]
            elif dx:
                dst = r["rows_in"].at[(dx + 1) // 2, c]
            else:
                dst = r["cols_in"].at[(dy + 1) // 2, c]
            copy = pltpu.make_async_remote_copy(
                field.at[rows, cols], dst, r["hssem"].at[2 * n + c], r["hrsem"].at[2 * n + c],
                device_id=at(dx, dy), device_id_type=MESH,
            )
            copy.start()
            copies.append(copy)

    shape = (32, 256)
    m2 = lax.broadcasted_iota(jnp.int32, shape, 0)
    cell = lax.broadcasted_iota(jnp.int32, shape, 1)
    kx = 4 * y_at + cell // 64 + 32 * m2
    ky = a // 4 + 8 * x_hi + 16 * ((a % 4) * 64 + cell % 64)
    wx = jnp.where(kx >= NX // 2, kx - NX, kx).astype(f32) * (2.0 * math.pi / NX)
    wy = jnp.where(ky >= NY // 2, ky - NY, ky).astype(f32) * (2.0 * math.pi / NY)
    den = wx * wx + wy * wy
    origin = (kx == 0) & (ky == 0)
    den = jnp.where(origin, 1.0, den)
    scale = 1.0 / (NX * NY)
    share = scale / den
    g_re = 0.5 * (wy * wy - wx * wx) * share
    g_im = jnp.where((kx == NX // 2) != (ky == NY // 2), 0.0, -(wx * wy) * share)
    r["gain"][0] = jnp.where(origin, 0.5 * scale, g_re)
    r["gain"][1] = jnp.where(origin, -0.5 * scale, g_re)
    r["gain"][2] = g_im

    for copy in copies:
        copy.wait_recv()
    surround(range(6), True)
    for i in (0, 8, 9):
        layer_1(i)
    layer_1_ends(range(1, 8))
    layer_2(
        [(0, PITCH), (7 * PITCH, 2 * PITCH)]
        + [(i * PITCH + 256 * end, 16) for i in range(1, 7) for end in range(2)]
    )

    s1, r1, st = r["s1"], r["r1"], r["st"]
    ssem, rsem = r["ssem"], r["rsem"]

    def block_of(step):
        return (y_at + far_first(step, 8)) % 8

    def third(i):
        start = pl.multiple_of(i * PITCH, 16)
        after = pl.multiple_of((i + 1) * PITCH, 16)
        return nt(k3[:, 0:256], x2[pl.ds(start, 384), :]) + nt(k3[:, 256:448], x2[pl.ds(after, 384), 0:192])

    def keep(y):
        y = y[0:80] + pltpu.roll(y[80:160], 383, 1) + pltpu.roll(y[160:240], 382, 1)
        for o in range(5):
            for k in range(3):
                cf[k, pl.ds(o, 16, stride=8), :] = y[o * 16 : o * 16 + 16, k * 128 : k * 128 + 128]

    def advance(i):
        def field_at(c, s, down, k):
            return fs[SHIFTS.index(s), c, k, pl.ds(4 * i + 7 + down, 8), :]

        flows = [[[], []] for _ in range(2)]
        for k in range(3):
            carry = (
                0.5 * (field_at(0, 1, 0, k) + field_at(0, 1, 1, k)),
                0.5 * (field_at(1, 1, 0, k) + field_at(1, 0, 0, k)),
            )
            for q in range(2):
                for d in range(2):
                    if d == 0:
                        taps = [field_at(q, 1, down, k) for down in (-1, 0, 1, 2)]
                    else:
                        taps = [field_at(q, s, 0, k) for s in (2, 1, 0, -1)]
                    base = 8 * d + 4 * q
                    weights = [cf[k, (base + s) * 8 : (base + s) * 8 + 8, :] + b3[base + s] for s in range(4)]
                    mean = 0.25 * ((weights[0] + weights[1]) + (weights[2] + weights[3]))
                    total = None
                    for s in range(4):
                        term = (stencil_base[s] + weights[s] - mean) * taps[s]
                        total = term if total is None else total + term
                    flows[d][q].append(carry[d] * total)
        for q in range(2):
            along_x = jnp.concatenate(flows[0][q], axis=1)
            along_y = jnp.concatenate(flows[1][q], axis=1)
            change = pltpu.roll(along_x + (along_y - pltpu.roll(along_y, 1, 1)), 7, 0) - along_x
            here = jnp.concatenate([field_at(q, 1, 1, k) for k in range(3)], axis=1)
            moved = pltpu.roll(here - step_ratio * change, 383, 1)
            for h in range(2):
                value = moved[0:4, h * 128 : h * 128 + 128]
                st[q * 2 + h, pl.ds(4 * i, 4), :] = value
                s1[i, q * 8 + h * 4 : q * 8 + h * 4 + 4, :] = value

    def send_block(i):
        for other in range(2):
            peer = 2 * i + other

            @pl.when(peer != b)
            def _():
                pltpu.make_async_remote_copy(
                    s1.at[i], r1.at[b], ssem.at[0], rsem.at[0], device_id={"gy": peer}, device_id_type=MESH
                ).start()

    def layer_3(step, _):
        y = third(block_of(step + 1))
        i = block_of(step)
        advance(i)
        keep(y)
        send_block(i)
        return 0

    keep(third(block_of(0)))
    lax.fori_loop(0, 7, layer_3, 0)
    advance(y_at)
    send_block(y_at)
    r1[b] = s1[y_at]

    def send(stage, axis, size, peer_of, src_of, dst):
        def go(step, _):
            peer = peer_of(step)
            pltpu.make_async_remote_copy(
                src_of(peer), dst, ssem.at[stage], rsem.at[stage], device_id={axis: peer}, device_id_type=MESH
            ).start()
            return 0

        lax.fori_loop(0, size - 1, go, 0)

    def x_peer(step):
        return (a + far_first(step, GX)) % GX

    def y_peer(step):
        return 2 * ((y_at + far_first(step, 8)) % 8) + x_hi

    def all_y_peer(step):
        return (b + far_first(step, GY)) % GY

    wait_for(rsem.at[0], r1.at[pl.ds(0, GY - 1)])

    tr, ti = r["tw"][x_hi, 0], r["tw"][x_hi, 1]
    x = jnp.concatenate(
        [
            jnp.concatenate([r1[:, c * 8 + h * 4 + i, :] for i in range(4) for h in range(2)], axis=1)
            for c in range(2)
        ],
        axis=0,
    )
    y = left_product(r["t_a"][x_hi], x)
    lines = []
    for i in range(4):
        yr, yi = y[:8, i * 256 : i * 256 + 256], y[8:, i * 256 : i * 256 + 256]
        lines.append(jnp.concatenate([yr * tr - yi * ti, yr * ti + yi * tr], axis=1))
    o = right_product(jnp.concatenate(lines, axis=0), r["t_b"])
    s2, r2 = r["s2"], r["r2"]
    for c in range(2):
        for rp in range(2):
            for h in range(2):
                cols = slice(c * 256 + h * 128, c * 256 + h * 128 + 128)
                pair = swap_halves(o[rp * 16 : rp * 16 + 8, cols], o[rp * 16 + 8 : rp * 16 + 16, cols], lane)
                for low in range(2):
                    s2[:, 2 * h + low, c * 2 + rp, :] = pair[low]
    send(1, "gx", GX, x_peer, lambda peer: s2.at[peer // 4, peer % 4], r2.at[a])
    r2[a] = s2[a // 4, a % 4]
    wait_for(rsem.at[1], r2.at[pl.ds(0, GX - 1)])

    x = jnp.concatenate(
        [jnp.concatenate([r2[:, c * 2 + rp, :] for rp in range(2)], axis=1) for c in range(2)], axis=0
    )
    y = left_product(r["t_s"][0], x)
    column = r["twr"][y_at]
    wide = lax.broadcasted_iota(jnp.int32, (32, 128), 1) < 64
    turns = [
        [jnp.where(wide, column[:, 4 * rp + c : 4 * rp + c + 1], column[:, 4 * rp + 2 + c : 4 * rp + 3 + c]) for c in range(2)]
        for rp in range(2)
    ]
    s3, r3 = r["s3"], r["r3"]
    for rp in range(2):
        cr, ci = turns[rp]
        yr, yi = y[:32, rp * 128 : rp * 128 + 128], y[32:, rp * 128 : rp * 128 + 128]
        for c, value in enumerate((yr * cr - yi * ci, yr * ci + yi * cr)):
            for tp in range(2):
                pair = swap_halves(value[tp * 16 : tp * 16 + 8], value[tp * 16 + 8 : tp * 16 + 16], lane)
                for low in range(2):
                    s3[:, c * 8 + (2 * rp + low) * 2 + tp, :] = pair[low]
    send(2, "gy", 8, y_peer, lambda peer: s3.at[peer // 2], r3.at[y_at])
    r3[y_at] = s3[y_at]
    wait_for(rsem.at[2], r3.at[pl.ds(0, 7)])
    x = jnp.concatenate(
        [
            jnp.concatenate([r3[:, c * 8 + i * 2 + tp, :] for tp in range(2)], axis=1)
            for c in range(2)
            for i in range(4)
        ],
        axis=0,
    )
    y = left_product(r["t_s"][1], x)
    yr, yi = y[:32], y[32:]

    gain = r["gain"]
    q = jnp.concatenate([gain[0] * yr - gain[2] * yi, -(gain[1] * yi + gain[2] * yr)], axis=0)

    y = left_product(r["t_s"][0], q)
    s4, r4 = r["s4"], r["r4"]
    for c in range(2):
        for i in range(4):
            for tp in range(2):
                row = c * 32 + i * 8
                s4[:, c * 8 + i * 2 + tp, :] = y[row : row + 8, tp * 128 : tp * 128 + 128]
    send(3, "gy", 8, y_peer, lambda peer: s4.at[peer // 2], r4.at[y_at])
    r4[y_at] = s4[y_at]
    wait_for(rsem.at[3], r4.at[pl.ds(0, 7)])
    halves = [[], []]
    for rp in range(2):
        cr, ci = turns[rp]
        parts = []
        for c in range(2):
            rows = []
            for tp in range(2):
                rows += swap_halves(r4[:, c * 8 + 4 * rp + tp, :], r4[:, c * 8 + 4 * rp + 2 + tp, :], lane)
            parts.append(jnp.concatenate(rows, axis=0))
        yr, yi = parts
        halves[0].append(yr * cr - yi * ci)
        halves[1].append(yr * ci + yi * cr)
    x = jnp.concatenate([jnp.concatenate(half, axis=1) for half in halves], axis=0)
    y = left_product(r["t_s"][1], x)
    s5, r5 = r["s5"], r["r5"]
    for c in range(2):
        for rp in range(2):
            s5[:, c * 2 + rp, :] = y[c * 32 : c * 32 + 32, rp * 128 : rp * 128 + 128]
    send(4, "gx", GX, x_peer, lambda peer: s5.at[peer], r5.at[a // 4, a % 4])
    r5[a // 4, a % 4] = s5[a]
    wait_for(rsem.at[4], s5.at[pl.ds(0, GX - 1)])
    lines = [[None] * 4 for _ in range(4)]
    for c in range(2):
        for rp in range(2):
            for h in range(2):
                pair = swap_halves(r5[:, 2 * h, c * 2 + rp, :], r5[:, 2 * h + 1, c * 2 + rp, :], lane)
                for low in range(2):
                    lines[2 * rp + low][c * 2 + h] = pair[low]
    x = jnp.concatenate([jnp.concatenate(line, axis=1) for line in lines], axis=0)
    o = right_product(x, r["t_b"])
    lines = [[], []]
    for i in range(4):
        yr, yi = o[i * 8 : i * 8 + 8, :256], o[i * 8 : i * 8 + 8, 256:]
        lines[0].append(yr * tr - yi * ti)
        lines[1].append(yr * ti + yi * tr)
    x = jnp.concatenate([jnp.concatenate(line, axis=1) for line in lines], axis=0)
    y = left_product(r["t_a2"][x_hi], x)
    s6, r6 = r["s6"], r["r6"]
    for c in range(2):
        for i in range(4):
            for h in range(2):
                at_lane = i * 256 + h * 128
                s6[:, c * 8 + h * 4 + i, :] = y[c * 16 : c * 16 + 16, at_lane : at_lane + 128]
    send(5, "gy", GY, all_y_peer, lambda peer: s6.at[peer], r6.at[y_at, x_hi])
    r6[y_at, x_hi] = s6[b]
    wait_for(rsem.at[5], s6.at[pl.ds(0, GY - 1)])
    back = r["back"]
    for c in range(2):
        for h in range(2):
            for i in range(4):
                index = c * 8 + h * 4 + i
                back[pl.ds(i, 8, stride=4), :] = r6[:, 0, index, :] + r6[:, 1, index, :]
            r["fields_next"][c, :, h * 128 : h * 128 + 128] = 0.5 * st[c * 2 + h] + back[...]

    for copy in copies:
        copy.wait_send()
    for stage, like in (
        (0, r1.at[pl.ds(0, GY - 1)]),
        (1, r2.at[pl.ds(0, GX - 1)]),
        (2, s3.at[pl.ds(0, 7)]),
        (3, s4.at[pl.ds(0, 7)]),
        (4, s5.at[pl.ds(0, GX - 1)]),
        (5, s6.at[pl.ds(0, GY - 1)]),
    ):
        wait_for(ssem.at[stage], like)


def on_device(u_field, v_field, w_first, b_first, w_second, b_second, w_third, b_third):
    inputs = {
        "u": u_field, "v": v_field, "w1": jnp.transpose(w_first, (0, 2, 1)), "w2": w_second, "w3": w_third,
        "b1": b_first[None], "b2": b_second[None], "b3": b_third,
    }
    inputs.update(zip(("t_a", "t_a2", "t_b", "tw", "t_s", "twr"), (jnp.asarray(t) for t in tables())))
    scratch = {
        name: (pltpu.SMEM if name == "b3" else pltpu.VMEM)(value.shape, value.dtype)
        for name, value in inputs.items()
    }
    scratch |= {
        "rows_in": pltpu.VMEM((2, 2, 8, 256), f32),
        "cols_in": pltpu.VMEM((2, 2, 32, 128), f32),
        "corner_in": pltpu.VMEM((2, 2, 2, 8, 128), f32),
        "fs": pltpu.VMEM((6, 2, 3, 56, 128), f32),
        "k1": pltpu.VMEM((48, 256), f32),
        "k2": pltpu.VMEM((3, 256, 384), bf16),
        "k3": pltpu.VMEM((240, 512), bf16),
        "x1": pltpu.VMEM((2, 10 * PITCH + 16, 128), f32),
        "x2": pltpu.VMEM((9 * PITCH + 384, 256), bf16),
        "cf": pltpu.VMEM((3, 128, 128), f32),
        "st": pltpu.VMEM((4, 32, 128), f32),
        "back": pltpu.VMEM((32, 128), f32),
        "gain": pltpu.VMEM((3, 32, 256), f32),
        "s1": pltpu.VMEM((8, 16, 128), f32),
        "r1": pltpu.VMEM((16, 16, 128), f32),
        "s2": pltpu.VMEM((8, 4, 4, 128), f32),
        "r2": pltpu.VMEM((32, 4, 128), f32),
        "s3": pltpu.VMEM((8, 16, 128), f32),
        "r3": pltpu.VMEM((8, 16, 128), f32),
        "s4": pltpu.VMEM((8, 16, 128), f32),
        "r4": pltpu.VMEM((8, 16, 128), f32),
        "s5": pltpu.VMEM((32, 4, 128), f32),
        "r5": pltpu.VMEM((8, 4, 4, 128), f32),
        "s6": pltpu.VMEM((16, 16, 128), f32),
        "r6": pltpu.VMEM((8, 2, 16, 128), f32),
        "lsem": pltpu.SemaphoreType.DMA((len(inputs),)),
        "hssem": pltpu.SemaphoreType.DMA((16,)),
        "hrsem": pltpu.SemaphoreType.DMA((16,)),
        "ssem": pltpu.SemaphoreType.DMA((6,)),
        "rsem": pltpu.SemaphoreType.DMA((6,)),
    }
    names = [name + "_hbm" for name in inputs] + ["fields_next"] + list(scratch)
    result = pl.pallas_call(
        functools.partial(kernel, names),
        out_shape=jax.ShapeDtypeStruct((2, 32, 256), f32),
        in_specs=[pl.BlockSpec(memory_space=pltpu.HBM)] * len(inputs),
        out_specs=pl.BlockSpec(memory_space=pltpu.VMEM),
        scratch_shapes=list(scratch.values()),
        compiler_params=pltpu.CompilerParams(collective_id=0, has_side_effects=True),
        name="step",
    )(*inputs.values())
    return result[0], result[1]


def solution(mesh):
    return jax.shard_map(
        on_device,
        mesh=mesh,
        in_specs=(P("gx", "gy"), P("gx", "gy"), P(), P(), P(), P(), P(), P()),
        out_specs=(P("gx", "gy"), P("gx", "gy")),
        check_vma=False,
    )
```

```python
import functools
import math

import jax
import jax.numpy as jnp
import ml_dtypes
import numpy as np
from jax import lax
from jax.experimental import pallas as pl
from jax.experimental.pallas import tpu as pltpu
from jax.sharding import PartitionSpec as P

step_ratio = 0.4
stencil_base = (-0.0625, 0.5625, 0.5625, -0.0625)
GX = 32
GY = 16
NX = 1024
NY = 4096
PITCH = 272
SHIFTS = (4, 3, 2, 1, 0, -1)
MESH = pl.DeviceIdType.MESH
f32 = jnp.float32
bf16 = jnp.bfloat16


def split_bf16(table):
    hi = table.astype(np.float32).astype(ml_dtypes.bfloat16)
    lo = (table - hi.astype(np.float64)).astype(np.float32).astype(ml_dtypes.bfloat16)
    return hi, lo


def real_left(matrix):
    return np.block([[matrix.real, -matrix.imag], [matrix.imag, matrix.real]])


def triple_left(table):
    hi, lo = split_bf16(table)
    return np.concatenate([hi, hi, lo], axis=1)


def root(product, whole):
    return np.exp(-2j * np.pi * (product % whole) / whole)


@functools.cache
def tables():
    n8, n16, n32, n256 = (np.arange(n) for n in (8, 16, 32, 256))
    paired = np.concatenate([4 * n8 + t for t in range(4)])
    sign = np.concatenate([np.ones(16), -np.ones(16)])
    halves = [n8, n8 + 8]
    t_a = np.stack([triple_left(real_left(root(np.outer(k, n16), 16)) * sign[None, :]) for k in halves])
    t_a2 = np.stack([triple_left(real_left(root(np.outer(n16, k), 16)) * sign[:, None]) for k in halves])
    mid = root(np.outer(n256, n256), 256)
    t_b = np.stack(split_bf16(np.block([[mid.real, mid.imag], [-mid.imag, mid.real]])))
    turn = [root(np.outer(k, n256), 4096) for k in halves]
    tw = np.stack([np.stack([w.real, w.imag]) for w in turn]).astype(np.float32)
    t_s = np.stack(
        [
            triple_left(real_left(root(np.outer(paired, n32), 32))),
            triple_left(real_left(root(np.outer(n32, paired), 32))),
        ]
    )
    twr = np.zeros((8, 32, 8), np.float32)
    for r in range(4):
        row = root(np.outer(4 * n8 + r, paired), 1024)
        twr[:, :, 2 * r] = row.real
        twr[:, :, 2 * r + 1] = row.imag
    return t_a, t_a2, t_b, tw, t_s, twr


def triple(value):
    hi = value.astype(bf16)
    lo = (value - hi.astype(f32)).astype(bf16)
    return jnp.concatenate([hi, lo, hi], axis=0)


def left_product(table, value):
    return jnp.dot(table, triple(value), preferred_element_type=f32)


def right_product(value, t_b):
    rows = value.shape[0]
    hi = value.astype(bf16)
    lo = (value - hi.astype(f32)).astype(bf16)
    both = jnp.dot(jnp.concatenate([hi, lo], axis=0), t_b[0], preferred_element_type=f32)
    return both[:rows] + both[rows:] + jnp.dot(hi, t_b[1], preferred_element_type=f32)


def nt(left, right):
    return lax.dot_general(left, right, (((1,), (1,)), ((), ())), preferred_element_type=f32)


def swap_halves(low, high, lane):
    first = lane < 64
    return jnp.where(first, low, pltpu.roll(high, 64, 1)), jnp.where(first, pltpu.roll(low, 64, 1), high)


def far_first(step, size):
    half = (step + 1) // 2
    return size // 2 + half - 2 * half * (step % 2)


def wait_for(sem, like):
    pltpu.make_async_copy(like, like, sem).wait()


def kernel(names, *refs):
    r = dict(zip(names, refs))
    a = lax.axis_index("gx")
    b = lax.axis_index("gy")
    y_at, x_hi = b // 2, b % 2

    def x_peer(step):
        z = (a % 16 // 2 + far_first(step // 4, 8)) % 8
        x_lo = (a // 16 + 1 - step % 4 // 2) % 2
        return x_lo * 16 + z * 2 + (a + 1 - step % 2) % 2

    def y_peer(step):
        return 2 * ((y_at + far_first(step, 8)) % 8) + x_hi

    def all_y_peer(step):
        return 2 * ((y_at + far_first(step // 2, 8)) % 8) + (b + 1 - step % 2) % 2

    moves = [(-1, -1), (-1, 1), (1, -1), (1, 1), (0, -1), (0, 1), (-1, 0), (1, 0)]

    def at(dx, dy):
        return {"gx": (a + dx + GX) % GX, "gy": (b + dy + GY) % GY}

    barrier = pltpu.get_barrier_semaphore()
    for dx, dy in moves:
        if dx and dy:
            pl.semaphore_signal(barrier, inc=1, device_id=at(dx, dy), device_id_type=MESH)

    def greet_y(step, _):
        pl.semaphore_signal(barrier, inc=1, device_id={"gy": all_y_peer(step)}, device_id_type=MESH)
        return 0

    def greet_x(step, _):
        pl.semaphore_signal(barrier, inc=1, device_id={"gx": x_peer(step)}, device_id_type=MESH)
        return 0

    lax.fori_loop(0, GY - 1, greet_y, 0)
    lax.fori_loop(0, GX - 1, greet_x, 0)
    local = []
    for n, name in enumerate(("u", "v", "w1", "w2", "w3", "b1", "b2", "b3", "t_a", "t_a2", "t_b", "tw", "t_s", "twr")):
        copy = pltpu.make_async_copy(r[name + "_hbm"], r[name], r["lsem"].at[n])
        copy.start()
        local.append(copy)
    u, v = r["u"], r["v"]

    local[0].wait()
    local[1].wait()
    lane = lax.broadcasted_iota(jnp.int32, (8, 128), 1)

    cols_out, corner_out = r["cols_out"], r["corner_out"]
    for e in range(2):
        tile = slice(e * 128, e * 128 + 128)
        both = jnp.concatenate([u[:, tile], v[:, tile], jnp.zeros((64, 128), f32)], axis=0)
        cols_out[e] = jnp.transpose(both)[e * 120 : e * 120 + 8]
        for d in range(2):
            rows = slice(d * 24, d * 24 + 8)
            ends = (u[rows, tile], v[rows, tile])
            other = pltpu.roll(ends[1], 64, 1)
            corner_out[d, e] = jnp.where(lane < 64, *((other, ends[0]) if e else (ends[0], other)))

    pl.semaphore_wait(barrier, GX + GY + 2)

    copies = []

    def give(src, dst, dx, dy):
        n = len(copies)
        copy = pltpu.make_async_remote_copy(
            src, dst, r["hssem"].at[n], r["hrsem"].at[n], device_id=at(dx, dy), device_id_type=MESH
        )
        copy.start()
        copies.append(copy)

    for dx, dy in moves:
        d, e = (dx + 1) // 2, (dy + 1) // 2
        if dx and dy:
            give(corner_out.at[d, e], r["corner_in"].at[d, e], dx, dy)
        elif dy:
            give(cols_out.at[e], r["cols_in"].at[e], dx, dy)
        else:
            for c, field in enumerate((u, v)):
                give(field.at[pl.ds(d * 24, 8), :], r["rows_in"].at[d, c], dx, dy)

    k1, k2, k3, x1, x2, fs, cf = (r[n] for n in ("k1", "k2", "k3", "x1", "x2", "fs", "cf"))
    k1[...] = jnp.zeros_like(k1)
    k2[...] = jnp.zeros_like(k2)
    k3[...] = jnp.zeros_like(k3)
    for copy in local[2:]:
        copy.wait()
    w1, w2, w3, b3 = (r[n] for n in ("w1", "w2", "w3", "b3"))
    for dj in range(3):
        for dr in range(3):
            tap = 3 * dr + dj
            for o in range(5):
                x = o + dr
                row = dj * 80 + o * 16
                k3[row : row + 16, x * 64 : x * 64 + 64] = w3[tap]
                if o == 4:
                    continue
                for c in range(2):
                    row = (dj * 2 + c) * 8 + x
                    k1[row : row + 1, o * 64 : o * 64 + 64] = w1[tap, c : c + 1, :].astype(f32)
                k2[dj, o * 64 : o * 64 + 64, x * 64 : x * 64 + 64] = w2[tap]
    bias1 = jnp.concatenate([r["b1"][...]] * 4, axis=1)
    bias2 = jnp.concatenate([r["b2"][...]] * 4, axis=1)
    x1[:, pl.ds(10 * PITCH, 16), :] = jnp.zeros((2, 16, 128), f32)
    x2[pl.ds(9 * PITCH, 384), :] = jnp.zeros((384, 256), bf16)


    def surround(groups, sides):
        for c, field in enumerate((u, v)):
            for g in groups:
                if g in (0, 5):
                    e = 1 if g == 0 else 0
                    corner, rows_in = r["corner_in"], r["rows_in"]
                    ends = [pltpu.roll(corner[e, n], 64, 1) if c else corner[e, n] for n in range(2)]
                    tiles = [ends[1], rows_in[e, c, :, 0:128], rows_in[e, c, :, 128:256], ends[0]]
                else:
                    rows = slice(g * 8 - 8, g * 8)
                    tiles = [field[rows, 0:128], field[rows, 128:256]]
                    if sides:
                        near = slice(c * 32 + g * 8 - 8, c * 32 + g * 8)
                        tiles = [sides[1][near], *tiles, sides[0][near]]
                    else:
                        tiles = [tiles[1], *tiles, tiles[0]]
                for n, s in enumerate(SHIFTS):
                    turned = [pltpu.roll(tile, s % 128, 1) if s else tile for tile in tiles]
                    for k in range(3):
                        if s > 0:
                            value = jnp.where(lane < s, turned[k], turned[k + 1])
                        elif s < 0 and k < 2:
                            value = jnp.where(lane >= 128 + s, turned[k + 2], turned[k + 1])
                        else:
                            value = turned[k + 1]
                        fs[n, c, k, g * 8 : g * 8 + 8, :] = value

    first_weights = k1[...].astype(bf16)

    def patches(i, tiles):
        return [
            jnp.concatenate([fs[dj, c, k, pl.ds(4 * i + 4, 8), :] for k in tiles], axis=1)
            for dj in range(3)
            for c in range(2)
        ]

    def first(patch):
        y = lax.dot_general(
            patch.astype(bf16), first_weights, (((0,), (0,)), ((), ())), preferred_element_type=f32
        )
        return y

    def layer_1(i):
        y = first(jnp.concatenate(patches(i, range(3)), axis=0))
        y = jnp.maximum(y[:PITCH] + bias1, 0.0)
        x1[0, pl.ds(i * PITCH, PITCH), :] = y[:, :128]
        x1[1, pl.ds(i * PITCH, PITCH), :] = y[:, 128:]

    def layer_1_ends(blocks):
        wide = lax.broadcasted_iota(jnp.int32, (48, 128), 1) // 8
        slots = [(i, end) for i in blocks for end in range(2)]
        packed = jnp.zeros((48, 128), f32)
        for n, (i, end) in enumerate(slots):
            patch = jnp.concatenate(patches(i, [2 * end]), axis=0)
            packed = jnp.where(wide == n, pltpu.roll(patch, 8 * n, 1) if n else patch, packed)
        y = jnp.maximum(first(packed) + bias1, 0.0)
        for n, (i, end) in enumerate(slots):
            at_row = i * PITCH + 256 * end
            x1[0, pl.ds(at_row, 8), :] = y[8 * n : 8 * n + 8, :128]
            x1[1, pl.ds(at_row, 8), :] = y[8 * n : 8 * n + 8, 128:]

    def layer_2(stretches):
        def piece(half, offset):
            return jnp.concatenate(
                [x1[half, pl.ds(start + offset, length), :].astype(bf16) for start, length in stretches], axis=0
            )

        y = None
        for dj in range(3):
            left = jnp.concatenate([piece(0, dj), piece(1, dj)], axis=1)
            term = nt(left, k2[dj, :, 0:256])
            y = term if y is None else y + term
        left = jnp.concatenate([piece(0, PITCH), piece(0, PITCH + 1)], axis=1)
        y = y + nt(left, jnp.concatenate([k2[0, :, 256:384], k2[1, :, 256:384]], axis=1))
        y = y + nt(piece(0, PITCH + 2), k2[2, :, 256:384])
        y = jnp.maximum(y + bias2, 0.0).astype(bf16)
        row = 0
        for start, length in stretches:
            x2[pl.ds(start, length), :] = y[row : row + length]
            row += length

    surround(range(1, 5), None)
    for i in range(1, 8):
        layer_1(i)

    def inner(i, _):
        layer_2([(pl.multiple_of((3 * i + 1) * PITCH, 16), 3 * PITCH)])
        return 0

    lax.fori_loop(0, 2, inner, 0)

    shape = (32, 256)
    m2 = lax.broadcasted_iota(jnp.int32, shape, 0)
    cell = lax.broadcasted_iota(jnp.int32, shape, 1)
    kx = 4 * y_at + cell // 64 + 32 * m2
    ky = a // 4 + 8 * x_hi + 16 * ((a % 4) * 64 + cell % 64)
    wx = jnp.where(kx >= NX // 2, kx - NX, kx).astype(f32) * (2.0 * math.pi / NX)
    wy = jnp.where(ky >= NY // 2, ky - NY, ky).astype(f32) * (2.0 * math.pi / NY)
    den = wx * wx + wy * wy
    origin = (kx == 0) & (ky == 0)
    den = jnp.where(origin, 1.0, den)
    scale = 1.0 / (NX * NY)
    share = scale / den
    g_re = 0.5 * (wy * wy - wx * wx) * share
    g_im = jnp.where((kx == NX // 2) != (ky == NY // 2), 0.0, -(wx * wy) * share)
    r["gain"][0] = jnp.where(origin, 0.5 * scale, g_re)
    r["gain"][1] = jnp.where(origin, -0.5 * scale, g_re)
    r["gain"][2] = g_im

    for copy in copies:
        copy.wait_recv()
    rest = jnp.zeros((120, 128), f32)
    right = jnp.transpose(jnp.concatenate([r["cols_in"][0], rest], axis=0))
    left = jnp.transpose(jnp.concatenate([rest, r["cols_in"][1]], axis=0))
    surround(range(6), (right, left))
    for i in (0, 8, 9):
        layer_1(i)
    layer_1_ends(range(1, 8))
    layer_2(
        [(0, PITCH), (7 * PITCH, 2 * PITCH)]
        + [(i * PITCH + 256 * end, 16) for i in range(1, 7) for end in range(2)]
    )

    s1, r1, st = r["s1"], r["r1"], r["st"]
    ssem, rsem = r["ssem"], r["rsem"]

    def block_of(step):
        return (y_at + far_first(step, 8)) % 8

    def third(i):
        start = pl.multiple_of(i * PITCH, 16)
        after = pl.multiple_of((i + 1) * PITCH, 16)
        return nt(k3[:, 0:256], x2[pl.ds(start, 384), :]) + nt(k3[:, 256:448], x2[pl.ds(after, 384), 0:192])

    def keep(y):
        y = y[0:80] + pltpu.roll(y[80:160], 383, 1) + pltpu.roll(y[160:240], 382, 1)
        for o in range(5):
            for k in range(3):
                cf[k, pl.ds(o, 16, stride=8), :] = y[o * 16 : o * 16 + 16, k * 128 : k * 128 + 128]

    def advance(i):
        def field_at(c, s, down, k):
            return fs[SHIFTS.index(s), c, k, pl.ds(4 * i + 7 + down, 8), :]

        flows = [[[], []] for _ in range(2)]
        for k in range(3):
            carry = (
                0.5 * (field_at(0, 1, 0, k) + field_at(0, 1, 1, k)),
                0.5 * (field_at(1, 1, 0, k) + field_at(1, 0, 0, k)),
            )
            for q in range(2):
                for d in range(2):
                    if d == 0:
                        taps = [field_at(q, 1, down, k) for down in (-1, 0, 1, 2)]
                    else:
                        taps = [field_at(q, s, 0, k) for s in (2, 1, 0, -1)]
                    base = 8 * d + 4 * q
                    weights = [cf[k, (base + s) * 8 : (base + s) * 8 + 8, :] + b3[base + s] for s in range(4)]
                    mean = 0.25 * ((weights[0] + weights[1]) + (weights[2] + weights[3]))
                    total = None
                    for s in range(4):
                        term = (stencil_base[s] + weights[s] - mean) * taps[s]
                        total = term if total is None else total + term
                    flows[d][q].append(carry[d] * total)
        for q in range(2):
            along_x = jnp.concatenate(flows[0][q], axis=1)
            along_y = jnp.concatenate(flows[1][q], axis=1)
            change = pltpu.roll(along_x + (along_y - pltpu.roll(along_y, 1, 1)), 7, 0) - along_x
            here = jnp.concatenate([field_at(q, 1, 1, k) for k in range(3)], axis=1)
            moved = pltpu.roll(here - step_ratio * change, 383, 1)
            for h in range(2):
                value = moved[0:4, h * 128 : h * 128 + 128]
                st[q * 2 + h, pl.ds(4 * i, 4), :] = value
                s1[i, q * 8 + h * 4 : q * 8 + h * 4 + 4, :] = value

    def send_block(i):
        for other in range(2):
            peer = 2 * i + other

            @pl.when(peer != b)
            def _():
                pltpu.make_async_remote_copy(
                    s1.at[i], r1.at[b], ssem.at[0], rsem.at[0], device_id={"gy": peer}, device_id_type=MESH
                ).start()

    def layer_3(step, _):
        y = third(block_of(step + 1))
        i = block_of(step)
        advance(i)
        keep(y)
        send_block(i)
        return 0

    keep(third(block_of(0)))
    lax.fori_loop(0, 7, layer_3, 0)
    advance(y_at)
    send_block(y_at)
    r1[b] = s1[y_at]

    def send(stage, axis, size, peer_of, src_of, dst):
        def go(step, _):
            peer = peer_of(step)
            pltpu.make_async_remote_copy(
                src_of(peer), dst, ssem.at[stage], rsem.at[stage], device_id={axis: peer}, device_id_type=MESH
            ).start()
            return 0

        lax.fori_loop(0, size - 1, go, 0)

    wait_for(rsem.at[0], r1.at[pl.ds(0, GY - 1)])

    tr, ti = r["tw"][x_hi, 0], r["tw"][x_hi, 1]
    x = jnp.concatenate(
        [
            jnp.concatenate([r1[:, c * 8 + h * 4 + i, :] for i in range(4) for h in range(2)], axis=1)
            for c in range(2)
        ],
        axis=0,
    )
    y = left_product(r["t_a"][x_hi], x)
    lines = []
    for i in range(4):
        yr, yi = y[:8, i * 256 : i * 256 + 256], y[8:, i * 256 : i * 256 + 256]
        lines.append(jnp.concatenate([yr * tr - yi * ti, yr * ti + yi * tr], axis=1))
    o = right_product(jnp.concatenate(lines, axis=0), r["t_b"])
    s2, r2 = r["s2"], r["r2"]
    for c in range(2):
        for rp in range(2):
            for h in range(2):
                cols = slice(c * 256 + h * 128, c * 256 + h * 128 + 128)
                pair = swap_halves(o[rp * 16 : rp * 16 + 8, cols], o[rp * 16 + 8 : rp * 16 + 16, cols], lane)
                for low in range(2):
                    s2[:, 2 * h + low, c * 2 + rp, :] = pair[low]
    send(1, "gx", GX, x_peer, lambda peer: s2.at[peer // 4, peer % 4], r2.at[a])
    r2[a] = s2[a // 4, a % 4]
    wait_for(rsem.at[1], r2.at[pl.ds(0, GX - 1)])

    x = jnp.concatenate(
        [jnp.concatenate([r2[:, c * 2 + rp, :] for rp in range(2)], axis=1) for c in range(2)], axis=0
    )
    y = left_product(r["t_s"][0], x)
    column = r["twr"][y_at]
    wide = lax.broadcasted_iota(jnp.int32, (32, 128), 1) < 64
    turns = [
        [jnp.where(wide, column[:, 4 * rp + c : 4 * rp + c + 1], column[:, 4 * rp + 2 + c : 4 * rp + 3 + c]) for c in range(2)]
        for rp in range(2)
    ]
    s3, r3 = r["s3"], r["r3"]
    for rp in range(2):
        cr, ci = turns[rp]
        yr, yi = y[:32, rp * 128 : rp * 128 + 128], y[32:, rp * 128 : rp * 128 + 128]
        for c, value in enumerate((yr * cr - yi * ci, yr * ci + yi * cr)):
            for tp in range(2):
                pair = swap_halves(value[tp * 16 : tp * 16 + 8], value[tp * 16 + 8 : tp * 16 + 16], lane)
                for low in range(2):
                    s3[:, c * 8 + (2 * rp + low) * 2 + tp, :] = pair[low]
    send(2, "gy", 8, y_peer, lambda peer: s3.at[peer // 2], r3.at[y_at])
    r3[y_at] = s3[y_at]
    wait_for(rsem.at[2], r3.at[pl.ds(0, 7)])
    x = jnp.concatenate(
        [
            jnp.concatenate([r3[:, c * 8 + i * 2 + tp, :] for tp in range(2)], axis=1)
            for c in range(2)
            for i in range(4)
        ],
        axis=0,
    )
    y = left_product(r["t_s"][1], x)
    yr, yi = y[:32], y[32:]

    gain = r["gain"]
    q = jnp.concatenate([gain[0] * yr - gain[2] * yi, -(gain[1] * yi + gain[2] * yr)], axis=0)

    y = left_product(r["t_s"][0], q)
    s4, r4 = r["s4"], r["r4"]
    for c in range(2):
        for i in range(4):
            for tp in range(2):
                row = c * 32 + i * 8
                s4[:, c * 8 + i * 2 + tp, :] = y[row : row + 8, tp * 128 : tp * 128 + 128]
    send(3, "gy", 8, y_peer, lambda peer: s4.at[peer // 2], r4.at[y_at])
    r4[y_at] = s4[y_at]
    wait_for(rsem.at[3], r4.at[pl.ds(0, 7)])
    halves = [[], []]
    for rp in range(2):
        cr, ci = turns[rp]
        parts = []
        for c in range(2):
            rows = []
            for tp in range(2):
                rows += swap_halves(r4[:, c * 8 + 4 * rp + tp, :], r4[:, c * 8 + 4 * rp + 2 + tp, :], lane)
            parts.append(jnp.concatenate(rows, axis=0))
        yr, yi = parts
        halves[0].append(yr * cr - yi * ci)
        halves[1].append(yr * ci + yi * cr)
    x = jnp.concatenate([jnp.concatenate(half, axis=1) for half in halves], axis=0)
    y = left_product(r["t_s"][1], x)
    s5, r5 = r["s5"], r["r5"]
    for c in range(2):
        for rp in range(2):
            s5[:, c * 2 + rp, :] = y[c * 32 : c * 32 + 32, rp * 128 : rp * 128 + 128]
    send(4, "gx", GX, x_peer, lambda peer: s5.at[peer], r5.at[a // 4, a % 4])
    r5[a // 4, a % 4] = s5[a]
    wait_for(rsem.at[4], s5.at[pl.ds(0, GX - 1)])
    lines = [[None] * 4 for _ in range(4)]
    for c in range(2):
        for rp in range(2):
            for h in range(2):
                pair = swap_halves(r5[:, 2 * h, c * 2 + rp, :], r5[:, 2 * h + 1, c * 2 + rp, :], lane)
                for low in range(2):
                    lines[2 * rp + low][c * 2 + h] = pair[low]
    x = jnp.concatenate([jnp.concatenate(line, axis=1) for line in lines], axis=0)
    o = right_product(x, r["t_b"])
    lines = [[], []]
    for i in range(4):
        yr, yi = o[i * 8 : i * 8 + 8, :256], o[i * 8 : i * 8 + 8, 256:]
        lines[0].append(yr * tr - yi * ti)
        lines[1].append(yr * ti + yi * tr)
    x = jnp.concatenate([jnp.concatenate(line, axis=1) for line in lines], axis=0)
    y = left_product(r["t_a2"][x_hi], x)
    s6, r6 = r["s6"], r["r6"]
    for c in range(2):
        for i in range(4):
            for h in range(2):
                at_lane = i * 256 + h * 128
                s6[:, c * 8 + h * 4 + i, :] = y[c * 16 : c * 16 + 16, at_lane : at_lane + 128]
    send(5, "gy", GY, all_y_peer, lambda peer: s6.at[peer], r6.at[y_at, x_hi])
    r6[y_at, x_hi] = s6[b]
    wait_for(rsem.at[5], s6.at[pl.ds(0, GY - 1)])
    back = r["back"]
    for c in range(2):
        for h in range(2):
            for i in range(4):
                index = c * 8 + h * 4 + i
                back[pl.ds(i, 8, stride=4), :] = r6[:, 0, index, :] + r6[:, 1, index, :]
            r["fields_next"][c, :, h * 128 : h * 128 + 128] = 0.5 * st[c * 2 + h] + back[...]

    for copy in copies:
        copy.wait_send()
    for stage, like in (
        (0, r1.at[pl.ds(0, GY - 1)]),
        (1, r2.at[pl.ds(0, GX - 1)]),
        (2, s3.at[pl.ds(0, 7)]),
        (3, s4.at[pl.ds(0, 7)]),
        (4, s5.at[pl.ds(0, GX - 1)]),
        (5, s6.at[pl.ds(0, GY - 1)]),
    ):
        wait_for(ssem.at[stage], like)


def on_device(u_field, v_field, w_first, b_first, w_second, b_second, w_third, b_third):
    inputs = {
        "u": u_field, "v": v_field, "w1": jnp.transpose(w_first, (0, 2, 1)), "w2": w_second, "w3": w_third,
        "b1": b_first[None], "b2": b_second[None], "b3": b_third,
    }
    inputs.update(zip(("t_a", "t_a2", "t_b", "tw", "t_s", "twr"), (jnp.asarray(t) for t in tables())))
    scratch = {
        name: (pltpu.SMEM if name == "b3" else pltpu.VMEM)(value.shape, value.dtype)
        for name, value in inputs.items()
    }
    scratch |= {
        "rows_in": pltpu.VMEM((2, 2, 8, 256), f32),
        "cols_in": pltpu.VMEM((2, 8, 128), f32),
        "corner_in": pltpu.VMEM((2, 2, 8, 128), f32),
        "cols_out": pltpu.VMEM((2, 8, 128), f32),
        "corner_out": pltpu.VMEM((2, 2, 8, 128), f32),
        "fs": pltpu.VMEM((6, 2, 3, 56, 128), f32),
        "k1": pltpu.VMEM((48, 256), f32),
        "k2": pltpu.VMEM((3, 256, 384), bf16),
        "k3": pltpu.VMEM((240, 512), bf16),
        "x1": pltpu.VMEM((2, 10 * PITCH + 16, 128), f32),
        "x2": pltpu.VMEM((9 * PITCH + 384, 256), bf16),
        "cf": pltpu.VMEM((3, 128, 128), f32),
        "st": pltpu.VMEM((4, 32, 128), f32),
        "back": pltpu.VMEM((32, 128), f32),
        "gain": pltpu.VMEM((3, 32, 256), f32),
        "s1": pltpu.VMEM((8, 16, 128), f32),
        "r1": pltpu.VMEM((16, 16, 128), f32),
        "s2": pltpu.VMEM((8, 4, 4, 128), f32),
        "r2": pltpu.VMEM((32, 4, 128), f32),
        "s3": pltpu.VMEM((8, 16, 128), f32),
        "r3": pltpu.VMEM((8, 16, 128), f32),
        "s4": pltpu.VMEM((8, 16, 128), f32),
        "r4": pltpu.VMEM((8, 16, 128), f32),
        "s5": pltpu.VMEM((32, 4, 128), f32),
        "r5": pltpu.VMEM((8, 4, 4, 128), f32),
        "s6": pltpu.VMEM((16, 16, 128), f32),
        "r6": pltpu.VMEM((8, 2, 16, 128), f32),
        "lsem": pltpu.SemaphoreType.DMA((len(inputs),)),
        "hssem": pltpu.SemaphoreType.DMA((10,)),
        "hrsem": pltpu.SemaphoreType.DMA((10,)),
        "ssem": pltpu.SemaphoreType.DMA((6,)),
        "rsem": pltpu.SemaphoreType.DMA((6,)),
    }
    names = [name + "_hbm" for name in inputs] + ["fields_next"] + list(scratch)
    result = pl.pallas_call(
        functools.partial(kernel, names),
        out_shape=jax.ShapeDtypeStruct((2, 32, 256), f32),
        in_specs=[pl.BlockSpec(memory_space=pltpu.HBM)] * len(inputs),
        out_specs=pl.BlockSpec(memory_space=pltpu.VMEM),
        scratch_shapes=list(scratch.values()),
        compiler_params=pltpu.CompilerParams(collective_id=0, has_side_effects=True),
        name="step",
    )(*inputs.values())
    return result[0], result[1]


def solution(mesh):
    return jax.shard_map(
        on_device,
        mesh=mesh,
        in_specs=(P("gx", "gy"), P("gx", "gy"), P(), P(), P(), P(), P(), P()),
        out_specs=(P("gx", "gy"), P("gx", "gy")),
        check_vma=False,
    )
```

```python
import functools
import math

import jax
import jax.numpy as jnp
import ml_dtypes
import numpy as np
from jax import lax
from jax.experimental import pallas as pl
from jax.experimental.pallas import tpu as pltpu
from jax.sharding import PartitionSpec as P

step_ratio = 0.4
stencil_base = (-0.0625, 0.5625, 0.5625, -0.0625)
GX = 32
GY = 16
NX = 1024
NY = 4096
PITCH = 272
SHIFTS = (4, 3, 2, 1, 0, -1)
MESH = pl.DeviceIdType.MESH
f32 = jnp.float32
bf16 = jnp.bfloat16


def split_bf16(table):
    hi = table.astype(np.float32).astype(ml_dtypes.bfloat16)
    lo = (table - hi.astype(np.float64)).astype(np.float32).astype(ml_dtypes.bfloat16)
    return hi, lo


def real_left(matrix):
    return np.block([[matrix.real, -matrix.imag], [matrix.imag, matrix.real]])


def triple_left(table):
    hi, lo = split_bf16(table)
    return np.concatenate([hi, hi, lo], axis=1)


def root(product, whole):
    return np.exp(-2j * np.pi * (product % whole) / whole)


@functools.cache
def tables():
    n8, n16, n32, n256 = (np.arange(n) for n in (8, 16, 32, 256))
    paired = np.concatenate([4 * n8 + t for t in range(4)])
    sign = np.concatenate([np.ones(16), -np.ones(16)])
    halves = [n8, n8 + 8]
    t_a = np.stack([triple_left(real_left(root(np.outer(k, n16), 16)) * sign[None, :]) for k in halves])
    t_a2 = np.stack([triple_left(real_left(root(np.outer(n16, k), 16)) * sign[:, None]) for k in halves])
    mid = root(np.outer(n256, n256), 256)
    t_b = np.stack(split_bf16(np.concatenate([mid.real, mid.imag], axis=1)))
    turn = [root(np.outer(k, n256), 4096) for k in halves]
    tw = np.stack([np.stack([w.real, w.imag]) for w in turn]).astype(np.float32)
    t_s = np.stack(
        [
            triple_left(real_left(root(np.outer(paired, n32), 32))),
            triple_left(real_left(root(np.outer(n32, paired), 32))),
        ]
    )
    twr = np.zeros((8, 32, 8), np.float32)
    for r in range(4):
        row = root(np.outer(4 * n8 + r, paired), 1024)
        twr[:, :, 2 * r] = row.real
        twr[:, :, 2 * r + 1] = row.imag
    return t_a, t_a2, t_b, tw, t_s, twr


def triple(value):
    hi = value.astype(bf16)
    lo = (value - hi.astype(f32)).astype(bf16)
    return jnp.concatenate([hi, lo, hi], axis=0)


def left_product(table, value):
    return jnp.dot(table, triple(value), preferred_element_type=f32)


def right_product(re, im, t_b):
    rows = re.shape[0]
    value = jnp.concatenate([re, im], axis=0)
    hi = value.astype(bf16)
    lo = (value - hi.astype(f32)).astype(bf16)
    both = jnp.dot(jnp.concatenate([hi, lo], axis=0), t_b[0], preferred_element_type=f32)
    total = both[: 2 * rows] + both[2 * rows :] + jnp.dot(hi, t_b[1], preferred_element_type=f32)
    by_re, by_im = total[:, :256], total[:, 256:]
    return by_re[:rows] - by_im[rows:], by_im[:rows] + by_re[rows:]


def nt(left, right):
    return lax.dot_general(left, right, (((1,), (1,)), ((), ())), preferred_element_type=f32)


def swap_halves(low, high, lane):
    first = lane < 64
    return jnp.where(first, low, pltpu.roll(high, 64, 1)), jnp.where(first, pltpu.roll(low, 64, 1), high)


def far_first(step, size):
    half = (step + 1) // 2
    return size // 2 + half - 2 * half * (step % 2)


def wait_for(sem, like):
    pltpu.make_async_copy(like, like, sem).wait()


def kernel(names, *refs):
    r = dict(zip(names, refs))
    a = lax.axis_index("gx")
    b = lax.axis_index("gy")
    y_at, x_hi = b // 2, b % 2

    z_at, core, x_lo = a % 16 // 2, a % 2, a // 16
    mates = [(1 - x_lo) * 16 + 1 - core, (1 - x_lo) * 16 + core, x_lo * 16 + 1 - core, x_lo * 16 + core]

    def each_x(go):
        def some(step, _):
            z = (z_at + far_first(step, 8)) % 8
            for end in mates:
                go(end + 2 * z)
            return 0

        lax.fori_loop(0, 7, some, 0)
        for end in mates[:3]:
            go(end + 2 * z_at)

    def each_y(go):
        def some(step, _):
            y = (y_at + far_first(step, 8)) % 8
            go(2 * y + 1 - x_hi)
            go(2 * y + x_hi)
            return 0

        lax.fori_loop(0, 7, some, 0)
        go(2 * y_at + 1 - x_hi)

    def each_near_y(go):
        def some(step, _):
            go(2 * ((y_at + far_first(step, 8)) % 8) + x_hi)
            return 0

        lax.fori_loop(0, 7, some, 0)

    moves = [(-1, -1), (-1, 1), (1, -1), (1, 1), (0, -1), (0, 1), (-1, 0), (1, 0)]

    def at(dx, dy):
        return {"gx": (a + dx + GX) % GX, "gy": (b + dy + GY) % GY}

    barrier = pltpu.get_barrier_semaphore()
    for dx, dy in moves:
        if dx and dy:
            pl.semaphore_signal(barrier, inc=1, device_id=at(dx, dy), device_id_type=MESH)

    def greet(axis):
        return lambda peer: pl.semaphore_signal(barrier, inc=1, device_id={axis: peer}, device_id_type=MESH)

    each_y(greet("gy"))
    each_x(greet("gx"))
    local = []
    for n, name in enumerate(("u", "v", "w1", "w2", "w3", "b1", "b2", "b3", "t_a", "t_a2", "t_b", "tw", "t_s", "twr")):
        copy = pltpu.make_async_copy(r[name + "_hbm"], r[name], r["lsem"].at[n])
        copy.start()
        local.append(copy)
    u, v = r["u"], r["v"]

    local[0].wait()
    local[1].wait()
    lane = lax.broadcasted_iota(jnp.int32, (8, 128), 1)

    cols_out, corner_out = r["cols_out"], r["corner_out"]
    for e in range(2):
        tile = slice(e * 128, e * 128 + 128)
        both = jnp.concatenate([u[:, tile], v[:, tile], jnp.zeros((64, 128), f32)], axis=0)
        cols_out[e] = jnp.transpose(both)[e * 120 : e * 120 + 8]
        for d in range(2):
            rows = slice(d * 24, d * 24 + 8)
            ends = (u[rows, tile], v[rows, tile])
            other = pltpu.roll(ends[1], 64, 1)
            corner_out[d, e] = jnp.where(lane < 64, *((other, ends[0]) if e else (ends[0], other)))

    pl.semaphore_wait(barrier, GX + GY + 2)

    copies = []

    def give(src, dst, dx, dy):
        n = len(copies)
        copy = pltpu.make_async_remote_copy(
            src, dst, r["hssem"].at[n], r["hrsem"].at[n], device_id=at(dx, dy), device_id_type=MESH
        )
        copy.start()
        copies.append(copy)

    for dx, dy in moves:
        d, e = (dx + 1) // 2, (dy + 1) // 2
        if dx and dy:
            give(corner_out.at[d, e], r["corner_in"].at[d, e], dx, dy)
        elif dy:
            give(cols_out.at[e], r["cols_in"].at[e], dx, dy)
        else:
            for c, field in enumerate((u, v)):
                give(field.at[pl.ds(d * 24, 8), :], r["rows_in"].at[d, c], dx, dy)

    k1, k2, k3, x1, x2, fs, cf = (r[n] for n in ("k1", "k2", "k3", "x1", "x2", "fs", "cf"))
    k1[...] = jnp.zeros_like(k1)
    k2[...] = jnp.zeros_like(k2)
    k3[...] = jnp.zeros_like(k3)
    for copy in local[2:]:
        copy.wait()
    w1, w2, w3, b3 = (r[n] for n in ("w1", "w2", "w3", "b3"))
    for dj in range(3):
        for dr in range(3):
            tap = 3 * dr + dj
            for o in range(5):
                x = o + dr
                row = dj * 80 + o * 16
                k3[row : row + 16, x * 64 : x * 64 + 64] = w3[tap]
                if o == 4:
                    continue
                for c in range(2):
                    row = (dj * 2 + c) * 8 + x
                    k1[row : row + 1, o * 64 : o * 64 + 64] = w1[tap, c : c + 1, :].astype(f32)
                k2[dj, o * 64 : o * 64 + 64, x * 64 : x * 64 + 64] = w2[tap]
    bias1 = jnp.concatenate([r["b1"][...]] * 4, axis=1)
    bias2 = jnp.concatenate([r["b2"][...]] * 4, axis=1)
    x1[:, pl.ds(10 * PITCH, 16), :] = jnp.zeros((2, 16, 128), f32)
    x2[pl.ds(9 * PITCH, 384), :] = jnp.zeros((384, 256), bf16)


    def surround(groups, sides):
        for c, field in enumerate((u, v)):
            for g in groups:
                if g in (0, 5):
                    e = 1 if g == 0 else 0
                    corner, rows_in = r["corner_in"], r["rows_in"]
                    ends = [pltpu.roll(corner[e, n], 64, 1) if c else corner[e, n] for n in range(2)]
                    tiles = [ends[1], rows_in[e, c, :, 0:128], rows_in[e, c, :, 128:256], ends[0]]
                else:
                    rows = slice(g * 8 - 8, g * 8)
                    tiles = [field[rows, 0:128], field[rows, 128:256]]
                    if sides:
                        near = slice(c * 32 + g * 8 - 8, c * 32 + g * 8)
                        tiles = [sides[1][near], *tiles, sides[0][near]]
                    else:
                        tiles = [tiles[1], *tiles, tiles[0]]
                for n, s in enumerate(SHIFTS):
                    turned = [pltpu.roll(tile, s % 128, 1) if s else tile for tile in tiles]
                    for k in range(3):
                        if s > 0:
                            value = jnp.where(lane < s, turned[k], turned[k + 1])
                        elif s < 0 and k < 2:
                            value = jnp.where(lane >= 128 + s, turned[k + 2], turned[k + 1])
                        else:
                            value = turned[k + 1]
                        fs[n, c, k, g * 8 : g * 8 + 8, :] = value

    first_weights = k1[...].astype(bf16)

    def patches(i, tiles):
        return [
            jnp.concatenate([fs[dj, c, k, pl.ds(4 * i + 4, 8), :] for k in tiles], axis=1)
            for dj in range(3)
            for c in range(2)
        ]

    def first(patch):
        y = lax.dot_general(
            patch.astype(bf16), first_weights, (((0,), (0,)), ((), ())), preferred_element_type=f32
        )
        return y

    def layer_1(i):
        y = first(jnp.concatenate(patches(i, range(3)), axis=0))
        y = jnp.maximum(y[:PITCH] + bias1, 0.0)
        x1[0, pl.ds(i * PITCH, PITCH), :] = y[:, :128]
        x1[1, pl.ds(i * PITCH, PITCH), :] = y[:, 128:]

    def layer_1_ends(blocks):
        wide = lax.broadcasted_iota(jnp.int32, (48, 128), 1) // 8
        slots = [(i, end) for i in blocks for end in range(2)]
        packed = jnp.zeros((48, 128), f32)
        for n, (i, end) in enumerate(slots):
            patch = jnp.concatenate(patches(i, [2 * end]), axis=0)
            packed = jnp.where(wide == n, pltpu.roll(patch, 8 * n, 1) if n else patch, packed)
        y = jnp.maximum(first(packed) + bias1, 0.0)
        for n, (i, end) in enumerate(slots):
            at_row = i * PITCH + 256 * end
            x1[0, pl.ds(at_row, 8), :] = y[8 * n : 8 * n + 8, :128]
            x1[1, pl.ds(at_row, 8), :] = y[8 * n : 8 * n + 8, 128:]

    def layer_2(stretches):
        def piece(half, offset):
            return jnp.concatenate(
                [x1[half, pl.ds(start + offset, length), :].astype(bf16) for start, length in stretches], axis=0
            )

        y = None
        for dj in range(3):
            left = jnp.concatenate([piece(0, dj), piece(1, dj)], axis=1)
            term = nt(left, k2[dj, :, 0:256])
            y = term if y is None else y + term
        left = jnp.concatenate([piece(0, PITCH), piece(0, PITCH + 1)], axis=1)
        y = y + nt(left, jnp.concatenate([k2[0, :, 256:384], k2[1, :, 256:384]], axis=1))
        y = y + nt(piece(0, PITCH + 2), k2[2, :, 256:384])
        y = jnp.maximum(y + bias2, 0.0).astype(bf16)
        row = 0
        for start, length in stretches:
            x2[pl.ds(start, length), :] = y[row : row + length]
            row += length

    surround(range(1, 5), None)
    for i in range(1, 8):
        layer_1(i)

    def inner(i, _):
        layer_2([(pl.multiple_of((3 * i + 1) * PITCH, 16), 3 * PITCH)])
        return 0

    lax.fori_loop(0, 2, inner, 0)

    shape = (32, 256)
    m2 = lax.broadcasted_iota(jnp.int32, shape, 0)
    cell = lax.broadcasted_iota(jnp.int32, shape, 1)
    kx = 4 * y_at + cell // 64 + 32 * m2
    ky = a // 4 + 8 * x_hi + 16 * ((a % 4) * 64 + cell % 64)
    wx = jnp.where(kx >= NX // 2, kx - NX, kx).astype(f32) * (2.0 * math.pi / NX)
    wy = jnp.where(ky >= NY // 2, ky - NY, ky).astype(f32) * (2.0 * math.pi / NY)
    den = wx * wx + wy * wy
    origin = (kx == 0) & (ky == 0)
    den = jnp.where(origin, 1.0, den)
    scale = 1.0 / (NX * NY)
    share = scale / den
    g_re = 0.5 * (wy * wy - wx * wx) * share
    g_im = jnp.where((kx == NX // 2) != (ky == NY // 2), 0.0, -(wx * wy) * share)
    r["gain"][0] = jnp.where(origin, 0.5 * scale, g_re)
    r["gain"][1] = jnp.where(origin, -0.5 * scale, g_re)
    r["gain"][2] = g_im

    for copy in copies:
        copy.wait_recv()
    rest = jnp.zeros((120, 128), f32)
    right = jnp.transpose(jnp.concatenate([r["cols_in"][0], rest], axis=0))
    left = jnp.transpose(jnp.concatenate([rest, r["cols_in"][1]], axis=0))
    surround(range(6), (right, left))
    for i in (0, 8, 9):
        layer_1(i)
    layer_1_ends(range(1, 8))
    layer_2(
        [(0, PITCH), (7 * PITCH, 2 * PITCH)]
        + [(i * PITCH + 256 * end, 16) for i in range(1, 7) for end in range(2)]
    )

    s1, r1, st = r["s1"], r["r1"], r["st"]
    ssem, rsem = r["ssem"], r["rsem"]

    def block_of(step):
        return (y_at + far_first(step, 8)) % 8

    def third(i):
        start = pl.multiple_of(i * PITCH, 16)
        after = pl.multiple_of((i + 1) * PITCH, 16)
        return nt(k3[:, 0:256], x2[pl.ds(start, 384), :]) + nt(k3[:, 256:448], x2[pl.ds(after, 384), 0:192])

    def keep(y):
        y = y[0:80] + pltpu.roll(y[80:160], 383, 1) + pltpu.roll(y[160:240], 382, 1)
        for o in range(5):
            for k in range(3):
                cf[k, pl.ds(o, 16, stride=8), :] = y[o * 16 : o * 16 + 16, k * 128 : k * 128 + 128]

    def advance(i):
        def field_at(c, s, down, k):
            return fs[SHIFTS.index(s), c, k, pl.ds(4 * i + 7 + down, 8), :]

        flows = [[[], []] for _ in range(2)]
        for k in range(3):
            carry = (
                0.5 * (field_at(0, 1, 0, k) + field_at(0, 1, 1, k)),
                0.5 * (field_at(1, 1, 0, k) + field_at(1, 0, 0, k)),
            )
            for q in range(2):
                for d in range(2):
                    if d == 0:
                        taps = [field_at(q, 1, down, k) for down in (-1, 0, 1, 2)]
                    else:
                        taps = [field_at(q, s, 0, k) for s in (2, 1, 0, -1)]
                    base = 8 * d + 4 * q
                    weights = [cf[k, (base + s) * 8 : (base + s) * 8 + 8, :] + b3[base + s] for s in range(4)]
                    mean = 0.25 * ((weights[0] + weights[1]) + (weights[2] + weights[3]))
                    total = None
                    for s in range(4):
                        term = (stencil_base[s] + weights[s] - mean) * taps[s]
                        total = term if total is None else total + term
                    flows[d][q].append(carry[d] * total)
        for q in range(2):
            along_x = jnp.concatenate(flows[0][q], axis=1)
            along_y = jnp.concatenate(flows[1][q], axis=1)
            change = pltpu.roll(along_x + (along_y - pltpu.roll(along_y, 1, 1)), 7, 0) - along_x
            here = jnp.concatenate([field_at(q, 1, 1, k) for k in range(3)], axis=1)
            moved = pltpu.roll(here - step_ratio * change, 383, 1)
            for h in range(2):
                value = moved[0:4, h * 128 : h * 128 + 128]
                st[q * 2 + h, pl.ds(4 * i, 4), :] = value
                s1[i, q * 8 + h * 4 : q * 8 + h * 4 + 4, :] = value

    def send_block(i):
        for other in range(2):
            peer = 2 * i + other

            @pl.when(peer != b)
            def _():
                pltpu.make_async_remote_copy(
                    s1.at[i], r1.at[b], ssem.at[0], rsem.at[0], device_id={"gy": peer}, device_id_type=MESH
                ).start()

    def layer_3(step, _):
        y = third(block_of(step + 1))
        i = block_of(step)
        advance(i)
        keep(y)
        send_block(i)
        return 0

    keep(third(block_of(0)))
    lax.fori_loop(0, 7, layer_3, 0)
    advance(y_at)
    send_block(y_at)
    r1[b] = s1[y_at]

    def send(stage, axis, each, src_of, dst):
        def go(peer):
            pltpu.make_async_remote_copy(
                src_of(peer), dst, ssem.at[stage], rsem.at[stage], device_id={axis: peer}, device_id_type=MESH
            ).start()

        each(go)

    wait_for(rsem.at[0], r1.at[pl.ds(0, GY - 1)])

    tr, ti = r["tw"][x_hi, 0], r["tw"][x_hi, 1]
    x = jnp.concatenate(
        [
            jnp.concatenate([r1[:, c * 8 + h * 4 + i, :] for i in range(4) for h in range(2)], axis=1)
            for c in range(2)
        ],
        axis=0,
    )
    y = left_product(r["t_a"][x_hi], x)
    lines = [[], []]
    for i in range(4):
        yr, yi = y[:8, i * 256 : i * 256 + 256], y[8:, i * 256 : i * 256 + 256]
        lines[0].append(yr * tr - yi * ti)
        lines[1].append(yr * ti + yi * tr)
    o = right_product(*(jnp.concatenate(line, axis=0) for line in lines), r["t_b"])
    s2, r2 = r["s2"], r["r2"]
    for c in range(2):
        for rp in range(2):
            for h in range(2):
                part = o[c][rp * 16 : rp * 16 + 16, h * 128 : h * 128 + 128]
                pair = swap_halves(part[:8], part[8:], lane)
                for low in range(2):
                    s2[:, 2 * h + low, c * 2 + rp, :] = pair[low]
    send(1, "gx", each_x, lambda peer: s2.at[peer // 4, peer % 4], r2.at[a])
    r2[a] = s2[a // 4, a % 4]
    wait_for(rsem.at[1], r2.at[pl.ds(0, GX - 1)])

    x = jnp.concatenate(
        [jnp.concatenate([r2[:, c * 2 + rp, :] for rp in range(2)], axis=1) for c in range(2)], axis=0
    )
    y = left_product(r["t_s"][0], x)
    column = r["twr"][y_at]
    wide = lax.broadcasted_iota(jnp.int32, (32, 128), 1) < 64
    turns = [
        [jnp.where(wide, column[:, 4 * rp + c : 4 * rp + c + 1], column[:, 4 * rp + 2 + c : 4 * rp + 3 + c]) for c in range(2)]
        for rp in range(2)
    ]
    s3, r3 = r["s3"], r["r3"]
    for rp in range(2):
        cr, ci = turns[rp]
        yr, yi = y[:32, rp * 128 : rp * 128 + 128], y[32:, rp * 128 : rp * 128 + 128]
        for c, value in enumerate((yr * cr - yi * ci, yr * ci + yi * cr)):
            for tp in range(2):
                pair = swap_halves(value[tp * 16 : tp * 16 + 8], value[tp * 16 + 8 : tp * 16 + 16], lane)
                for low in range(2):
                    s3[:, c * 8 + (2 * rp + low) * 2 + tp, :] = pair[low]
    send(2, "gy", each_near_y, lambda peer: s3.at[peer // 2], r3.at[y_at])
    r3[y_at] = s3[y_at]
    wait_for(rsem.at[2], r3.at[pl.ds(0, 7)])
    x = jnp.concatenate(
        [
            jnp.concatenate([r3[:, c * 8 + i * 2 + tp, :] for tp in range(2)], axis=1)
            for c in range(2)
            for i in range(4)
        ],
        axis=0,
    )
    y = left_product(r["t_s"][1], x)
    yr, yi = y[:32], y[32:]

    gain = r["gain"]
    q = jnp.concatenate([gain[0] * yr - gain[2] * yi, -(gain[1] * yi + gain[2] * yr)], axis=0)

    y = left_product(r["t_s"][0], q)
    s4, r4 = r["s4"], r["r4"]
    for c in range(2):
        for i in range(4):
            for tp in range(2):
                row = c * 32 + i * 8
                s4[:, c * 8 + i * 2 + tp, :] = y[row : row + 8, tp * 128 : tp * 128 + 128]
    send(3, "gy", each_near_y, lambda peer: s4.at[peer // 2], r4.at[y_at])
    r4[y_at] = s4[y_at]
    wait_for(rsem.at[3], r4.at[pl.ds(0, 7)])
    halves = [[], []]
    for rp in range(2):
        cr, ci = turns[rp]
        parts = []
        for c in range(2):
            rows = []
            for tp in range(2):
                rows += swap_halves(r4[:, c * 8 + 4 * rp + tp, :], r4[:, c * 8 + 4 * rp + 2 + tp, :], lane)
            parts.append(jnp.concatenate(rows, axis=0))
        yr, yi = parts
        halves[0].append(yr * cr - yi * ci)
        halves[1].append(yr * ci + yi * cr)
    x = jnp.concatenate([jnp.concatenate(half, axis=1) for half in halves], axis=0)
    y = left_product(r["t_s"][1], x)
    s5, r5 = r["s5"], r["r5"]
    for c in range(2):
        for rp in range(2):
            s5[:, c * 2 + rp, :] = y[c * 32 : c * 32 + 32, rp * 128 : rp * 128 + 128]
    send(4, "gx", each_x, lambda peer: s5.at[peer], r5.at[a // 4, a % 4])
    r5[a // 4, a % 4] = s5[a]
    wait_for(rsem.at[4], s5.at[pl.ds(0, GX - 1)])
    lines = [[None] * 4 for _ in range(4)]
    for c in range(2):
        for rp in range(2):
            for h in range(2):
                pair = swap_halves(r5[:, 2 * h, c * 2 + rp, :], r5[:, 2 * h + 1, c * 2 + rp, :], lane)
                for low in range(2):
                    lines[2 * rp + low][c * 2 + h] = pair[low]
    x = [
        jnp.concatenate([jnp.concatenate(line[c * 2 : c * 2 + 2], axis=1) for line in lines], axis=0)
        for c in range(2)
    ]
    o = right_product(*x, r["t_b"])
    lines = [[], []]
    for i in range(4):
        yr, yi = o[0][i * 8 : i * 8 + 8], o[1][i * 8 : i * 8 + 8]
        lines[0].append(yr * tr - yi * ti)
        lines[1].append(yr * ti + yi * tr)
    x = jnp.concatenate([jnp.concatenate(line, axis=1) for line in lines], axis=0)
    y = left_product(r["t_a2"][x_hi], x)
    s6, r6 = r["s6"], r["r6"]
    for c in range(2):
        for i in range(4):
            for h in range(2):
                at_lane = i * 256 + h * 128
                s6[:, c * 8 + h * 4 + i, :] = y[c * 16 : c * 16 + 16, at_lane : at_lane + 128]
    send(5, "gy", each_y, lambda peer: s6.at[peer], r6.at[y_at, x_hi])
    r6[y_at, x_hi] = s6[b]
    wait_for(rsem.at[5], s6.at[pl.ds(0, GY - 1)])
    back = r["back"]
    for c in range(2):
        for h in range(2):
            for i in range(4):
                index = c * 8 + h * 4 + i
                back[pl.ds(i, 8, stride=4), :] = r6[:, 0, index, :] + r6[:, 1, index, :]
            r["fields_next"][c, :, h * 128 : h * 128 + 128] = 0.5 * st[c * 2 + h] + back[...]

    for copy in copies:
        copy.wait_send()
    for stage, like in (
        (0, r1.at[pl.ds(0, GY - 1)]),
        (1, r2.at[pl.ds(0, GX - 1)]),
        (2, s3.at[pl.ds(0, 7)]),
        (3, s4.at[pl.ds(0, 7)]),
        (4, s5.at[pl.ds(0, GX - 1)]),
        (5, s6.at[pl.ds(0, GY - 1)]),
    ):
        wait_for(ssem.at[stage], like)


def on_device(u_field, v_field, w_first, b_first, w_second, b_second, w_third, b_third):
    inputs = {
        "u": u_field, "v": v_field, "w1": jnp.transpose(w_first, (0, 2, 1)), "w2": w_second, "w3": w_third,
        "b1": b_first[None], "b2": b_second[None], "b3": b_third,
    }
    inputs.update(zip(("t_a", "t_a2", "t_b", "tw", "t_s", "twr"), (jnp.asarray(t) for t in tables())))
    scratch = {
        name: (pltpu.SMEM if name == "b3" else pltpu.VMEM)(value.shape, value.dtype)
        for name, value in inputs.items()
    }
    scratch |= {
        "rows_in": pltpu.VMEM((2, 2, 8, 256), f32),
        "cols_in": pltpu.VMEM((2, 8, 128), f32),
        "corner_in": pltpu.VMEM((2, 2, 8, 128), f32),
        "cols_out": pltpu.VMEM((2, 8, 128), f32),
        "corner_out": pltpu.VMEM((2, 2, 8, 128), f32),
        "fs": pltpu.VMEM((6, 2, 3, 56, 128), f32),
        "k1": pltpu.VMEM((48, 256), f32),
        "k2": pltpu.VMEM((3, 256, 384), bf16),
        "k3": pltpu.VMEM((240, 512), bf16),
        "x1": pltpu.VMEM((2, 10 * PITCH + 16, 128), f32),
        "x2": pltpu.VMEM((9 * PITCH + 384, 256), bf16),
        "cf": pltpu.VMEM((3, 128, 128), f32),
        "st": pltpu.VMEM((4, 32, 128), f32),
        "back": pltpu.VMEM((32, 128), f32),
        "gain": pltpu.VMEM((3, 32, 256), f32),
        "s1": pltpu.VMEM((8, 16, 128), f32),
        "r1": pltpu.VMEM((16, 16, 128), f32),
        "s2": pltpu.VMEM((8, 4, 4, 128), f32),
        "r2": pltpu.VMEM((32, 4, 128), f32),
        "s3": pltpu.VMEM((8, 16, 128), f32),
        "r3": pltpu.VMEM((8, 16, 128), f32),
        "s4": pltpu.VMEM((8, 16, 128), f32),
        "r4": pltpu.VMEM((8, 16, 128), f32),
        "s5": pltpu.VMEM((32, 4, 128), f32),
        "r5": pltpu.VMEM((8, 4, 4, 128), f32),
        "s6": pltpu.VMEM((16, 16, 128), f32),
        "r6": pltpu.VMEM((8, 2, 16, 128), f32),
        "lsem": pltpu.SemaphoreType.DMA((len(inputs),)),
        "hssem": pltpu.SemaphoreType.DMA((10,)),
        "hrsem": pltpu.SemaphoreType.DMA((10,)),
        "ssem": pltpu.SemaphoreType.DMA((6,)),
        "rsem": pltpu.SemaphoreType.DMA((6,)),
    }
    names = [name + "_hbm" for name in inputs] + ["fields_next"] + list(scratch)
    result = pl.pallas_call(
        functools.partial(kernel, names),
        out_shape=jax.ShapeDtypeStruct((2, 32, 256), f32),
        in_specs=[pl.BlockSpec(memory_space=pltpu.HBM)] * len(inputs),
        out_specs=pl.BlockSpec(memory_space=pltpu.VMEM),
        scratch_shapes=list(scratch.values()),
        compiler_params=pltpu.CompilerParams(collective_id=0, has_side_effects=True),
        name="step",
    )(*inputs.values())
    return result[0], result[1]


def solution(mesh):
    return jax.shard_map(
        on_device,
        mesh=mesh,
        in_specs=(P("gx", "gy"), P("gx", "gy"), P(), P(), P(), P(), P(), P()),
        out_specs=(P("gx", "gy"), P("gx", "gy")),
        check_vma=False,
    )
```

```python
import functools
import math

import jax
import jax.numpy as jnp
import ml_dtypes
import numpy as np
from jax import lax
from jax.experimental import pallas as pl
from jax.experimental.pallas import tpu as pltpu
from jax.sharding import PartitionSpec as P

step_ratio = 0.4
stencil_base = (-0.0625, 0.5625, 0.5625, -0.0625)
GX = 32
GY = 16
NX = 1024
NY = 4096
PITCH = 272
SHIFTS = (4, 3, 2, 1, 0, -1)
MESH = pl.DeviceIdType.MESH
f32 = jnp.float32
bf16 = jnp.bfloat16


def split_bf16(table):
    hi = table.astype(np.float32).astype(ml_dtypes.bfloat16)
    lo = (table - hi.astype(np.float64)).astype(np.float32).astype(ml_dtypes.bfloat16)
    return hi, lo


def real_left(matrix):
    return np.block([[matrix.real, -matrix.imag], [matrix.imag, matrix.real]])


def triple_left(table):
    hi, lo = split_bf16(table)
    return np.concatenate([hi, hi, lo], axis=1)


def root(product, whole):
    return np.exp(-2j * np.pi * (product % whole) / whole)


@functools.cache
def tables():
    n8, n16, n32, n256 = (np.arange(n) for n in (8, 16, 32, 256))
    paired = np.concatenate([4 * n8 + t for t in range(4)])
    sign = np.concatenate([np.ones(16), -np.ones(16)])
    halves = [n8, n8 + 8]
    t_a = np.stack([triple_left(real_left(root(np.outer(k, n16), 16)) * sign[None, :]) for k in halves])
    t_a2 = np.stack([triple_left(real_left(root(np.outer(n16, k), 16)) * sign[:, None]) for k in halves])
    mid = root(np.outer(n256, n256), 256)
    t_b = np.stack(split_bf16(np.concatenate([mid.real, mid.imag], axis=1)))
    turn = [root(np.outer(k, n256), 4096) for k in halves]
    tw = np.stack([np.stack([w.real, w.imag]) for w in turn]).astype(np.float32)
    t_s = np.stack(
        [
            triple_left(real_left(root(np.outer(paired, n32), 32))),
            triple_left(real_left(root(np.outer(n32, paired), 32))),
        ]
    )
    twr = np.zeros((8, 32, 8), np.float32)
    for r in range(4):
        row = root(np.outer(4 * n8 + r, paired), 1024)
        twr[:, :, 2 * r] = row.real
        twr[:, :, 2 * r + 1] = row.imag
    return t_a, t_a2, t_b, tw, t_s, twr


def triple(value):
    hi = value.astype(bf16)
    lo = (value - hi.astype(f32)).astype(bf16)
    return jnp.concatenate([hi, lo, hi], axis=0)


def left_product(table, value):
    return jnp.dot(table, triple(value), preferred_element_type=f32)


def right_product(re, im, t_b):
    rows = re.shape[0]
    value = jnp.concatenate([re, im], axis=0)
    hi = value.astype(bf16)
    lo = (value - hi.astype(f32)).astype(bf16)
    both = jnp.dot(jnp.concatenate([hi, lo], axis=0), t_b[0], preferred_element_type=f32)
    total = both[: 2 * rows] + both[2 * rows :] + jnp.dot(hi, t_b[1], preferred_element_type=f32)
    by_re, by_im = total[:, :256], total[:, 256:]
    return by_re[:rows] - by_im[rows:], by_im[:rows] + by_re[rows:]


def nt(left, right):
    return lax.dot_general(left, right, (((1,), (1,)), ((), ())), preferred_element_type=f32)


def swap_halves(low, high, lane):
    first = lane < 64
    return jnp.where(first, low, pltpu.roll(high, 64, 1)), jnp.where(first, pltpu.roll(low, 64, 1), high)


def far_first(step, size):
    half = (step + 1) // 2
    return size // 2 + half - 2 * half * (step % 2)


def wait_for(sem, like):
    pltpu.make_async_copy(like, like, sem).wait()


def kernel(names, *refs):
    r = dict(zip(names, refs))
    a = lax.axis_index("gx")
    b = lax.axis_index("gy")
    y_at, x_hi = b // 2, b % 2

    z_at, core, x_lo = a % 16 // 2, a % 2, a // 16
    mates = [(1 - x_lo) * 16 + 1 - core, (1 - x_lo) * 16 + core, x_lo * 16 + 1 - core, x_lo * 16 + core]

    def each_x(go):
        def some(step, _):
            z = (z_at + far_first(step, 8)) % 8
            for end in mates:
                go(end + 2 * z)
            return 0

        lax.fori_loop(0, 7, some, 0)
        for end in mates[:3]:
            go(end + 2 * z_at)

    def each_y(go):
        def some(step, _):
            y = (y_at + far_first(step, 8)) % 8
            go(2 * y + 1 - x_hi)
            go(2 * y + x_hi)
            return 0

        lax.fori_loop(0, 7, some, 0)
        go(2 * y_at + 1 - x_hi)

    def each_near_y(go):
        def some(step, _):
            go(2 * ((y_at + far_first(step, 8)) % 8) + x_hi)
            return 0

        lax.fori_loop(0, 7, some, 0)

    moves = [(-1, -1), (-1, 1), (1, -1), (1, 1), (0, -1), (0, 1), (-1, 0), (1, 0)]

    def at(dx, dy):
        return {"gx": (a + dx + GX) % GX, "gy": (b + dy + GY) % GY}

    barrier = pltpu.get_barrier_semaphore()
    for dx, dy in moves:
        if dx and dy:
            pl.semaphore_signal(barrier, inc=1, device_id=at(dx, dy), device_id_type=MESH)

    def greet(axis):
        return lambda peer: pl.semaphore_signal(barrier, inc=1, device_id={axis: peer}, device_id_type=MESH)

    each_y(greet("gy"))
    each_x(greet("gx"))
    local = []
    for n, name in enumerate(("u", "v", "w1", "w2", "w3", "b1", "b2", "b3", "t_a", "t_a2", "t_b", "tw", "t_s", "twr")):
        copy = pltpu.make_async_copy(r[name + "_hbm"], r[name], r["lsem"].at[n])
        copy.start()
        local.append(copy)
    u, v = r["u"], r["v"]

    local[0].wait()
    local[1].wait()
    lane = lax.broadcasted_iota(jnp.int32, (8, 128), 1)

    cols_out, corner_out = r["cols_out"], r["corner_out"]
    for e in range(2):
        tile = slice(e * 128, e * 128 + 128)
        both = jnp.concatenate([u[:, tile], v[:, tile], jnp.zeros((64, 128), f32)], axis=0)
        cols_out[e] = jnp.transpose(both)[e * 120 : e * 120 + 8]
        for d in range(2):
            rows = slice(d * 24, d * 24 + 8)
            ends = (u[rows, tile], v[rows, tile])
            other = pltpu.roll(ends[1], 64, 1)
            corner_out[d, e] = jnp.where(lane < 64, *((other, ends[0]) if e else (ends[0], other)))

    pl.semaphore_wait(barrier, GX + GY + 2)

    copies = []

    def give(src, dst, dx, dy):
        n = len(copies)
        copy = pltpu.make_async_remote_copy(
            src, dst, r["hssem"].at[n], r["hrsem"].at[n], device_id=at(dx, dy), device_id_type=MESH
        )
        copy.start()
        copies.append(copy)

    for dx, dy in moves:
        d, e = (dx + 1) // 2, (dy + 1) // 2
        if dx and dy:
            give(corner_out.at[d, e], r["corner_in"].at[d, e], dx, dy)
        elif dy:
            give(cols_out.at[e], r["cols_in"].at[e], dx, dy)
        else:
            for c, field in enumerate((u, v)):
                give(field.at[pl.ds(d * 24, 8), :], r["rows_in"].at[d, c], dx, dy)

    k1, k2, k3, x1, x2, fs, cf = (r[n] for n in ("k1", "k2", "k3", "x1", "x2", "fs", "cf"))
    k1[...] = jnp.zeros_like(k1)
    k2[...] = jnp.zeros_like(k2)
    k3[...] = jnp.zeros_like(k3)
    for copy in local[2:]:
        copy.wait()
    w1, w2, w3, b3 = (r[n] for n in ("w1", "w2", "w3", "b3"))
    for dj in range(3):
        for dr in range(3):
            tap = 3 * dr + dj
            for o in range(5):
                x = o + dr
                row = dj * 80 + o * 16
                k3[row : row + 16, x * 64 : x * 64 + 64] = w3[tap]
                if o == 4:
                    continue
                for c in range(2):
                    row = (dj * 2 + c) * 8 + x
                    k1[row : row + 1, o * 64 : o * 64 + 64] = w1[tap, c : c + 1, :].astype(f32)
                k2[dj, o * 64 : o * 64 + 64, x * 64 : x * 64 + 64] = w2[tap]
    bias1 = jnp.concatenate([r["b1"][...]] * 4, axis=1)
    bias2 = jnp.concatenate([r["b2"][...]] * 4, axis=1)
    x1[:, pl.ds(10 * PITCH, 16), :] = jnp.zeros((2, 16, 128), f32)
    x2[pl.ds(9 * PITCH, 384), :] = jnp.zeros((384, 256), bf16)


    def surround(groups, sides):
        for c, field in enumerate((u, v)):
            for g in groups:
                if g in (0, 5):
                    e = 1 if g == 0 else 0
                    corner, rows_in = r["corner_in"], r["rows_in"]
                    ends = [pltpu.roll(corner[e, n], 64, 1) if c else corner[e, n] for n in range(2)]
                    tiles = [ends[1], rows_in[e, c, :, 0:128], rows_in[e, c, :, 128:256], ends[0]]
                else:
                    rows = slice(g * 8 - 8, g * 8)
                    tiles = [field[rows, 0:128], field[rows, 128:256]]
                    if sides:
                        near = slice(c * 32 + g * 8 - 8, c * 32 + g * 8)
                        tiles = [sides[1][near], *tiles, sides[0][near]]
                    else:
                        tiles = [tiles[1], *tiles, tiles[0]]
                for n, s in enumerate(SHIFTS):
                    turned = [pltpu.roll(tile, s % 128, 1) if s else tile for tile in tiles]
                    for k in range(3):
                        if s > 0:
                            value = jnp.where(lane < s, turned[k], turned[k + 1])
                        elif s < 0 and k < 2:
                            value = jnp.where(lane >= 128 + s, turned[k + 2], turned[k + 1])
                        else:
                            value = turned[k + 1]
                        fs[n, c, k, g * 8 : g * 8 + 8, :] = value

    first_weights = k1[...].astype(bf16)

    def patches(i, tiles):
        return [
            jnp.concatenate([fs[dj, c, k, pl.ds(4 * i + 4, 8), :] for k in tiles], axis=1)
            for dj in range(3)
            for c in range(2)
        ]

    def first(patch):
        y = lax.dot_general(
            patch.astype(bf16), first_weights, (((0,), (0,)), ((), ())), preferred_element_type=f32
        )
        return y

    def layer_1(i):
        y = first(jnp.concatenate(patches(i, range(3)), axis=0))
        y = jnp.maximum(y[:PITCH] + bias1, 0.0)
        x1[0, pl.ds(i * PITCH, PITCH), :] = y[:, :128]
        x1[1, pl.ds(i * PITCH, PITCH), :] = y[:, 128:]

    def layer_1_ends(blocks):
        wide = lax.broadcasted_iota(jnp.int32, (48, 128), 1) // 8
        slots = [(i, end) for i in blocks for end in range(2)]
        packed = jnp.zeros((48, 128), f32)
        for n, (i, end) in enumerate(slots):
            patch = jnp.concatenate(patches(i, [2 * end]), axis=0)
            packed = jnp.where(wide == n, pltpu.roll(patch, 8 * n, 1) if n else patch, packed)
        y = jnp.maximum(first(packed) + bias1, 0.0)
        for n, (i, end) in enumerate(slots):
            at_row = i * PITCH + 256 * end
            x1[0, pl.ds(at_row, 8), :] = y[8 * n : 8 * n + 8, :128]
            x1[1, pl.ds(at_row, 8), :] = y[8 * n : 8 * n + 8, 128:]

    def layer_2(stretches):
        def piece(half, offset):
            return jnp.concatenate(
                [x1[half, pl.ds(start + offset, length), :].astype(bf16) for start, length in stretches], axis=0
            )

        y = None
        for dj in range(3):
            left = jnp.concatenate([piece(0, dj), piece(1, dj)], axis=1)
            term = nt(left, k2[dj, :, 0:256])
            y = term if y is None else y + term
        left = jnp.concatenate([piece(0, PITCH), piece(0, PITCH + 1)], axis=1)
        y = y + nt(left, jnp.concatenate([k2[0, :, 256:384], k2[1, :, 256:384]], axis=1))
        y = y + nt(piece(0, PITCH + 2), k2[2, :, 256:384])
        y = jnp.maximum(y + bias2, 0.0).astype(bf16)
        row = 0
        for start, length in stretches:
            x2[pl.ds(start, length), :] = y[row : row + length]
            row += length

    surround(range(1, 5), None)
    for i in range(1, 8):
        layer_1(i)

    def inner(i, _):
        layer_2([(pl.multiple_of((3 * i + 1) * PITCH, 16), 3 * PITCH)])
        return 0

    lax.fori_loop(0, 2, inner, 0)

    shape = (32, 256)
    m2 = lax.broadcasted_iota(jnp.int32, shape, 0)
    cell = lax.broadcasted_iota(jnp.int32, shape, 1)
    kx = 4 * y_at + cell // 64 + 32 * m2
    ky = a // 4 + 8 * x_hi + 16 * ((a % 4) * 64 + cell % 64)
    wx = jnp.where(kx >= NX // 2, kx - NX, kx).astype(f32) * (2.0 * math.pi / NX)
    wy = jnp.where(ky >= NY // 2, ky - NY, ky).astype(f32) * (2.0 * math.pi / NY)
    den = wx * wx + wy * wy
    origin = (kx == 0) & (ky == 0)
    den = jnp.where(origin, 1.0, den)
    scale = 1.0 / (NX * NY)
    share = scale / den
    g_re = 0.5 * (wy * wy - wx * wx) * share
    g_im = jnp.where((kx == NX // 2) != (ky == NY // 2), 0.0, -(wx * wy) * share)
    r["gain"][0] = jnp.where(origin, 0.5 * scale, g_re)
    r["gain"][1] = jnp.where(origin, -0.5 * scale, g_re)
    r["gain"][2] = g_im

    for copy in copies:
        copy.wait_recv()
    rest = jnp.zeros((120, 128), f32)
    right = jnp.transpose(jnp.concatenate([r["cols_in"][0], rest], axis=0))
    left = jnp.transpose(jnp.concatenate([rest, r["cols_in"][1]], axis=0))
    surround(range(6), (right, left))
    for i in (0, 8, 9):
        layer_1(i)
    layer_1_ends(range(1, 8))
    layer_2(
        [(0, PITCH), (7 * PITCH, 2 * PITCH)]
        + [(i * PITCH + 256 * end, 16) for i in range(1, 7) for end in range(2)]
    )

    s1, r1, st = r["s1"], r["r1"], r["st"]
    ssem, rsem = r["ssem"], r["rsem"]

    def block_of(step):
        return (y_at + far_first(step, 8)) % 8

    def third(i):
        start = pl.multiple_of(i * PITCH, 16)
        after = pl.multiple_of((i + 1) * PITCH, 16)
        return nt(k3[:, 0:256], x2[pl.ds(start, 384), :]) + nt(k3[:, 256:448], x2[pl.ds(after, 384), 0:192])

    def keep(y):
        y = y[0:80] + pltpu.roll(y[80:160], 383, 1) + pltpu.roll(y[160:240], 382, 1)
        for o in range(5):
            for k in range(3):
                cf[k, pl.ds(o, 16, stride=8), :] = y[o * 16 : o * 16 + 16, k * 128 : k * 128 + 128]

    def advance(i):
        def field_at(c, s, down, k):
            return fs[SHIFTS.index(s), c, k, pl.ds(4 * i + 7 + down, 8), :]

        flows = [[[], []] for _ in range(2)]
        for k in range(3):
            carry = (
                0.5 * (field_at(0, 1, 0, k) + field_at(0, 1, 1, k)),
                0.5 * (field_at(1, 1, 0, k) + field_at(1, 0, 0, k)),
            )
            for q in range(2):
                for d in range(2):
                    if d == 0:
                        taps = [field_at(q, 1, down, k) for down in (-1, 0, 1, 2)]
                    else:
                        taps = [field_at(q, s, 0, k) for s in (2, 1, 0, -1)]
                    base = 8 * d + 4 * q
                    weights = [cf[k, (base + s) * 8 : (base + s) * 8 + 8, :] + b3[base + s] for s in range(4)]
                    mean = 0.25 * ((weights[0] + weights[1]) + (weights[2] + weights[3]))
                    total = None
                    for s in range(4):
                        term = (stencil_base[s] + weights[s] - mean) * taps[s]
                        total = term if total is None else total + term
                    flows[d][q].append(carry[d] * total)
        for q in range(2):
            along_x = jnp.concatenate(flows[0][q], axis=1)
            along_y = jnp.concatenate(flows[1][q], axis=1)
            change = pltpu.roll(along_x + (along_y - pltpu.roll(along_y, 1, 1)), 7, 0) - along_x
            here = jnp.concatenate([field_at(q, 1, 1, k) for k in range(3)], axis=1)
            moved = pltpu.roll(here - step_ratio * change, 383, 1)
            for h in range(2):
                value = moved[0:4, h * 128 : h * 128 + 128]
                st[q * 2 + h, pl.ds(4 * i, 4), :] = value
                s1[i, q * 8 + h * 4 : q * 8 + h * 4 + 4, :] = value

    def send_block(i):
        for other in range(2):
            peer = 2 * i + other

            @pl.when(peer != b)
            def _():
                pltpu.make_async_remote_copy(
                    s1.at[i], r1.at[b], ssem.at[0], rsem.at[0], device_id={"gy": peer}, device_id_type=MESH
                ).start()

    def layer_3(step, _):
        y = third(block_of(step + 1))
        i = block_of(step)
        advance(i)
        send_block(i)
        keep(y)
        return 0

    keep(third(block_of(0)))
    lax.fori_loop(0, 7, layer_3, 0)
    advance(y_at)
    send_block(y_at)
    r1[b] = s1[y_at]

    def send(stage, axis, each, src_of, dst):
        def go(peer):
            pltpu.make_async_remote_copy(
                src_of(peer), dst, ssem.at[stage], rsem.at[stage], device_id={axis: peer}, device_id_type=MESH
            ).start()

        each(go)

    wait_for(rsem.at[0], r1.at[pl.ds(0, GY - 1)])

    tr, ti = r["tw"][x_hi, 0], r["tw"][x_hi, 1]
    x = jnp.concatenate(
        [
            jnp.concatenate([r1[:, c * 8 + h * 4 + i, :] for i in range(4) for h in range(2)], axis=1)
            for c in range(2)
        ],
        axis=0,
    )
    y = left_product(r["t_a"][x_hi], x)
    lines = [[], []]
    for i in range(4):
        yr, yi = y[:8, i * 256 : i * 256 + 256], y[8:, i * 256 : i * 256 + 256]
        lines[0].append(yr * tr - yi * ti)
        lines[1].append(yr * ti + yi * tr)
    o = right_product(*(jnp.concatenate(line, axis=0) for line in lines), r["t_b"])
    s2, r2 = r["s2"], r["r2"]
    for c in range(2):
        for rp in range(2):
            for h in range(2):
                part = o[c][rp * 16 : rp * 16 + 16, h * 128 : h * 128 + 128]
                pair = swap_halves(part[:8], part[8:], lane)
                for low in range(2):
                    s2[:, 2 * h + low, c * 2 + rp, :] = pair[low]
    send(1, "gx", each_x, lambda peer: s2.at[peer // 4, peer % 4], r2.at[a])
    r2[a] = s2[a // 4, a % 4]
    wait_for(rsem.at[1], r2.at[pl.ds(0, GX - 1)])

    x = jnp.concatenate(
        [jnp.concatenate([r2[:, c * 2 + rp, :] for rp in range(2)], axis=1) for c in range(2)], axis=0
    )
    y = left_product(r["t_s"][0], x)
    column = r["twr"][y_at]
    wide = lax.broadcasted_iota(jnp.int32, (32, 128), 1) < 64
    turns = [
        [jnp.where(wide, column[:, 4 * rp + c : 4 * rp + c + 1], column[:, 4 * rp + 2 + c : 4 * rp + 3 + c]) for c in range(2)]
        for rp in range(2)
    ]
    s3, r3 = r["s3"], r["r3"]
    for rp in range(2):
        cr, ci = turns[rp]
        yr, yi = y[:32, rp * 128 : rp * 128 + 128], y[32:, rp * 128 : rp * 128 + 128]
        for c, value in enumerate((yr * cr - yi * ci, yr * ci + yi * cr)):
            for tp in range(2):
                pair = swap_halves(value[tp * 16 : tp * 16 + 8], value[tp * 16 + 8 : tp * 16 + 16], lane)
                for low in range(2):
                    s3[:, c * 8 + (2 * rp + low) * 2 + tp, :] = pair[low]
    send(2, "gy", each_near_y, lambda peer: s3.at[peer // 2], r3.at[y_at])
    r3[y_at] = s3[y_at]
    wait_for(rsem.at[2], r3.at[pl.ds(0, 7)])
    x = jnp.concatenate(
        [
            jnp.concatenate([r3[:, c * 8 + i * 2 + tp, :] for tp in range(2)], axis=1)
            for c in range(2)
            for i in range(4)
        ],
        axis=0,
    )
    y = left_product(r["t_s"][1], x)
    yr, yi = y[:32], y[32:]

    gain = r["gain"]
    q = jnp.concatenate([gain[0] * yr - gain[2] * yi, -(gain[1] * yi + gain[2] * yr)], axis=0)

    y = left_product(r["t_s"][0], q)
    s4, r4 = r["s4"], r["r4"]
    for c in range(2):
        for i in range(4):
            for tp in range(2):
                row = c * 32 + i * 8
                s4[:, c * 8 + i * 2 + tp, :] = y[row : row + 8, tp * 128 : tp * 128 + 128]
    send(3, "gy", each_near_y, lambda peer: s4.at[peer // 2], r4.at[y_at])
    r4[y_at] = s4[y_at]
    wait_for(rsem.at[3], r4.at[pl.ds(0, 7)])
    halves = [[], []]
    for rp in range(2):
        cr, ci = turns[rp]
        parts = []
        for c in range(2):
            rows = []
            for tp in range(2):
                rows += swap_halves(r4[:, c * 8 + 4 * rp + tp, :], r4[:, c * 8 + 4 * rp + 2 + tp, :], lane)
            parts.append(jnp.concatenate(rows, axis=0))
        yr, yi = parts
        halves[0].append(yr * cr - yi * ci)
        halves[1].append(yr * ci + yi * cr)
    x = jnp.concatenate([jnp.concatenate(half, axis=1) for half in halves], axis=0)
    y = left_product(r["t_s"][1], x)
    s5, r5 = r["s5"], r["r5"]
    for c in range(2):
        for rp in range(2):
            s5[:, c * 2 + rp, :] = y[c * 32 : c * 32 + 32, rp * 128 : rp * 128 + 128]
    send(4, "gx", each_x, lambda peer: s5.at[peer], r5.at[a // 4, a % 4])
    r5[a // 4, a % 4] = s5[a]
    wait_for(rsem.at[4], s5.at[pl.ds(0, GX - 1)])
    lines = [[None] * 4 for _ in range(4)]
    for c in range(2):
        for rp in range(2):
            for h in range(2):
                pair = swap_halves(r5[:, 2 * h, c * 2 + rp, :], r5[:, 2 * h + 1, c * 2 + rp, :], lane)
                for low in range(2):
                    lines[2 * rp + low][c * 2 + h] = pair[low]
    x = [
        jnp.concatenate([jnp.concatenate(line[c * 2 : c * 2 + 2], axis=1) for line in lines], axis=0)
        for c in range(2)
    ]
    o = right_product(*x, r["t_b"])
    lines = [[], []]
    for i in range(4):
        yr, yi = o[0][i * 8 : i * 8 + 8], o[1][i * 8 : i * 8 + 8]
        lines[0].append(yr * tr - yi * ti)
        lines[1].append(yr * ti + yi * tr)
    x = jnp.concatenate([jnp.concatenate(line, axis=1) for line in lines], axis=0)
    y = left_product(r["t_a2"][x_hi], x)
    s6, r6 = r["s6"], r["r6"]
    for c in range(2):
        for i in range(4):
            for h in range(2):
                at_lane = i * 256 + h * 128
                s6[:, c * 8 + h * 4 + i, :] = y[c * 16 : c * 16 + 16, at_lane : at_lane + 128]
    send(5, "gy", each_y, lambda peer: s6.at[peer], r6.at[y_at, x_hi])
    r6[y_at, x_hi] = s6[b]
    wait_for(rsem.at[5], s6.at[pl.ds(0, GY - 1)])
    back = r["back"]
    for c in range(2):
        for h in range(2):
            for i in range(4):
                index = c * 8 + h * 4 + i
                back[pl.ds(i, 8, stride=4), :] = r6[:, 0, index, :] + r6[:, 1, index, :]
            r["fields_next"][c, :, h * 128 : h * 128 + 128] = 0.5 * st[c * 2 + h] + back[...]

    for copy in copies:
        copy.wait_send()
    for stage, like in (
        (0, r1.at[pl.ds(0, GY - 1)]),
        (1, r2.at[pl.ds(0, GX - 1)]),
        (2, s3.at[pl.ds(0, 7)]),
        (3, s4.at[pl.ds(0, 7)]),
        (4, s5.at[pl.ds(0, GX - 1)]),
        (5, s6.at[pl.ds(0, GY - 1)]),
    ):
        wait_for(ssem.at[stage], like)


def on_device(u_field, v_field, w_first, b_first, w_second, b_second, w_third, b_third):
    inputs = {
        "u": u_field, "v": v_field, "w1": jnp.transpose(w_first, (0, 2, 1)), "w2": w_second, "w3": w_third,
        "b1": b_first[None], "b2": b_second[None], "b3": b_third,
    }
    inputs.update(zip(("t_a", "t_a2", "t_b", "tw", "t_s", "twr"), (jnp.asarray(t) for t in tables())))
    scratch = {
        name: (pltpu.SMEM if name == "b3" else pltpu.VMEM)(value.shape, value.dtype)
        for name, value in inputs.items()
    }
    scratch |= {
        "rows_in": pltpu.VMEM((2, 2, 8, 256), f32),
        "cols_in": pltpu.VMEM((2, 8, 128), f32),
        "corner_in": pltpu.VMEM((2, 2, 8, 128), f32),
        "cols_out": pltpu.VMEM((2, 8, 128), f32),
        "corner_out": pltpu.VMEM((2, 2, 8, 128), f32),
        "fs": pltpu.VMEM((6, 2, 3, 56, 128), f32),
        "k1": pltpu.VMEM((48, 256), f32),
        "k2": pltpu.VMEM((3, 256, 384), bf16),
        "k3": pltpu.VMEM((240, 512), bf16),
        "x1": pltpu.VMEM((2, 10 * PITCH + 16, 128), f32),
        "x2": pltpu.VMEM((9 * PITCH + 384, 256), bf16),
        "cf": pltpu.VMEM((3, 128, 128), f32),
        "st": pltpu.VMEM((4, 32, 128), f32),
        "back": pltpu.VMEM((32, 128), f32),
        "gain": pltpu.VMEM((3, 32, 256), f32),
        "s1": pltpu.VMEM((8, 16, 128), f32),
        "r1": pltpu.VMEM((16, 16, 128), f32),
        "s2": pltpu.VMEM((8, 4, 4, 128), f32),
        "r2": pltpu.VMEM((32, 4, 128), f32),
        "s3": pltpu.VMEM((8, 16, 128), f32),
        "r3": pltpu.VMEM((8, 16, 128), f32),
        "s4": pltpu.VMEM((8, 16, 128), f32),
        "r4": pltpu.VMEM((8, 16, 128), f32),
        "s5": pltpu.VMEM((32, 4, 128), f32),
        "r5": pltpu.VMEM((8, 4, 4, 128), f32),
        "s6": pltpu.VMEM((16, 16, 128), f32),
        "r6": pltpu.VMEM((8, 2, 16, 128), f32),
        "lsem": pltpu.SemaphoreType.DMA((len(inputs),)),
        "hssem": pltpu.SemaphoreType.DMA((10,)),
        "hrsem": pltpu.SemaphoreType.DMA((10,)),
        "ssem": pltpu.SemaphoreType.DMA((6,)),
        "rsem": pltpu.SemaphoreType.DMA((6,)),
    }
    names = [name + "_hbm" for name in inputs] + ["fields_next"] + list(scratch)
    result = pl.pallas_call(
        functools.partial(kernel, names),
        out_shape=jax.ShapeDtypeStruct((2, 32, 256), f32),
        in_specs=[pl.BlockSpec(memory_space=pltpu.HBM)] * len(inputs),
        out_specs=pl.BlockSpec(memory_space=pltpu.VMEM),
        scratch_shapes=list(scratch.values()),
        compiler_params=pltpu.CompilerParams(collective_id=0, has_side_effects=True),
        name="step",
    )(*inputs.values())
    return result[0], result[1]


def solution(mesh):
    return jax.shard_map(
        on_device,
        mesh=mesh,
        in_specs=(P("gx", "gy"), P("gx", "gy"), P(), P(), P(), P(), P(), P()),
        out_specs=(P("gx", "gy"), P("gx", "gy")),
        check_vma=False,
    )
```
